256 devices in a mesh: section: 4 (over x_lo, core), seq: 16 (over x_hi, z), dp: 4 (over y).
Axes of the slice: x: 4 (x_hi: 2, x_lo: 2; x = x_hi * 2 + x_lo), y: 4, z: 8, core: 2. Of those that a mesh axis runs over, the one named last changes fastest.
Arguments:
- tile_feats: bfloat16 [4, 8192, 1536], P('dp', 'seq', 'section'), may hold values from -6 to 6
- tile_gain: float32 [1536], replicated, may hold values from 0.25 to 1.75
- w_gate: bfloat16 [1536, 4096], P(('seq', 'dp'), 'section'), may hold values from -0.15625 to 0.15625
- w_up: bfloat16 [1536, 4096], P(('seq', 'dp'), 'section'), may hold values from -0.15625 to 0.15625
- w_down: bfloat16 [4096, 1536], P('section', ('seq', 'dp')), may hold values from -0.09375 to 0.09375
- w_proj: bfloat16 [1536, 768], P('section'), may hold values from -0.15625 to 0.15625
- slide_gain: float32 [768], replicated, may hold values from 0.25 to 1.75
- w_qkv: bfloat16 [3, 768, 768], P(None, None, 'section'), may hold values from -0.7647408 to 0.7647408
- w_out: bfloat16 [768, 768], P('section'), may hold values from -0.21875 to 0.21875
- lengths: int32 [4, 3], P('dp'), may hold values from 1 to 6144, 8192 in all within a row
- seg_len: int32 [16], P('section'), may hold values from 512 to 8192
- rate: int32 [16], P('section'), may hold values from 1 to 4
Outputs:
- slide_out: bfloat16 [4, 8192, 768], P('dp', 'seq', 'section')
The draws below stay inside these ranges and needn't reach their ends.
Inputs may be any that keep to these rules, and one draw needn't show every extreme that they name: Each row of lengths sums to 8192, and one slide of each pack has 6144 tiles.
All inputs are finite; a program needn't handle non-finite values.
Results may differ from the reference program's by a relative error of at most 0.0087.
Values may be sent and summed in bfloat16 or wider, within the bound.
A program may use at most 192 MiB of HBM per device.

```python
import math
import jax
import jax.numpy as jnp
import numpy as np
from jax import lax

TILE_D = 1536
TILE_FF = 4096
HEADS = 16
HEAD_DIM = 48
TOK_DEV = 512
SLIDES = 3
SLIDE_D = 768
SEQ = 8192
PACKS = 4


def draw_w_qkv(key, part):
    streams = jax.random.split(jax.random.fold_in(key, 7), 6)
    background = jax.random.truncated_normal(streams[0], -4.0, 4.0, (3, SLIDE_D, SLIDE_D), jnp.float32) / math.sqrt(SLIDE_D)
    lowest, highest = (3.0, 8.0)
    choose = jax.random.randint(streams[1], (HEADS // 2,), 0, 2)
    strong_head = jnp.stack([choose == 0, choose == 1], axis=1).reshape(HEADS)
    strong = jnp.exp(jax.random.uniform(streams[2], (HEADS,), jnp.float32, math.log(lowest), math.log(highest)))
    gentle = jnp.exp(jax.random.uniform(streams[3], (HEADS,), jnp.float32, math.log(0.3), math.log(2.0)))
    strength = jnp.where(strong_head, strong, gentle)
    amplitude = jnp.sqrt(strength / math.sqrt(HEAD_DIM))
    direction = jax.random.truncated_normal(streams[4], -4.0, 4.0, (SLIDE_D, HEADS), jnp.float32) / math.sqrt(SLIDE_D)
    pattern = jax.random.truncated_normal(streams[5], -4.0, 4.0, (HEADS, HEAD_DIM), jnp.float32)
    planted = (direction[:, :, None] * (amplitude[:, None] * pattern)[None, :, :]).reshape(SLIDE_D, HEADS * HEAD_DIM)
    nothing = jnp.zeros_like(planted)
    return (background + jnp.stack([planted, planted, nothing])).astype(jnp.bfloat16)


def plant(result, own_key, low, largest):
    longest = result.shape.index(max(result.shape))
    spots = []
    for shift in (0, 1):
        where = [jax.random.randint(jax.random.fold_in(own_key, axis), (), 0, length) for axis, length in enumerate(result.shape)]
        where[longest] = (where[longest] + shift) % result.shape[longest]
        spots.append(tuple(where))
    return result.at[spots[0]].set(low).at[spots[1]].set(largest)


def level_of(key, extent, pieces, least, top_value):
    level = 1.0
    for position, parts in pieces:
        draws = jax.random.uniform(jax.random.fold_in(jax.random.fold_in(key, 6), position), (parts,), jnp.float32, least / len(pieces), top_value / len(pieces))
        level = level * jnp.repeat(jnp.exp(draws), extent[position] // parts).reshape((-1,) + (1,) * (len(extent) - 1 - position))
    return level


def profile(amount, total, limit, lean):
    portions = [(1 << 20) // math.isqrt(rank ** lean) + 1 for rank in range(2, amount + 1)]
    spare, counts = total - limit - (amount - 1), [1] * (amount - 1)
    while spare > 0:
        candidates = [i for i in range(amount - 1) if counts[i] < limit]
        pool, left = sum([portions[i] for i in candidates]), spare
        for i in candidates:
            extra = min(limit - counts[i], max(1, left * portions[i] // pool), spare)
            counts[i] = counts[i] + extra
            spare = spare - extra
    return np.array([limit] + counts)


def uneven(rng, amount, total, bound, slope):
    if amount == 2:
        one = jax.random.randint(rng, (), max(1, total - bound), min(bound, total - 1) + 1)
        return jnp.stack([one, total - one])
    sizes = jnp.asarray(profile(amount, total, bound, slope), jnp.int32)
    couples = (amount - 1) // 2
    source_of, receiver = sizes[1:1 + 2 * couples:2], sizes[2:2 + 2 * couples:2]
    margin = jnp.minimum(source_of - 1, bound - receiver)
    shifted = jax.random.randint(jax.random.fold_in(rng, 1), (couples,), 0, 1 << 20) % (margin + 1)
    sizes = sizes.at[1:1 + 2 * couples:2].set(source_of - shifted).at[2:2 + 2 * couples:2].set(receiver + shifted)
    return sizes[jax.random.permutation(jax.random.fold_in(rng, 2), amount)]


def normal_values(key, dims, deviation, limit, cuts=(), kind=jnp.bfloat16):
    entries = jax.random.normal(key, dims, jnp.float32) * deviation
    if len(cuts) > 0:
        entries = level_of(key, dims, cuts, -0.22, 0.18) * entries
    return jnp.clip(entries, min=-limit, max=limit).astype(kind)


def setup_inputs(seed: int = 0) -> dict:
    arg_keys = jax.random.split(jax.random.key(seed), 13)
    tile_feats = normal_values(arg_keys[0], (PACKS, SEQ, TILE_D), 1.0, 6.0, ((0, 4), (1, 16), (2, 4)))
    tile_gain = jnp.clip(1.0 + 0.15 * jax.random.normal(arg_keys[1], (TILE_D,), jnp.float32), 0.25, 1.75)
    w_gate = normal_values(arg_keys[2], (TILE_D, TILE_FF), TILE_D ** -0.5, 0.15625, ((0, 64), (1, 4)))
    w_up = normal_values(arg_keys[3], (TILE_D, TILE_FF), TILE_D ** -0.5, 0.15625, ((0, 64), (1, 4)))
    w_down = normal_values(arg_keys[4], (TILE_FF, TILE_D), TILE_FF ** -0.5, 0.09375, ((0, 4), (1, 64)))
    w_proj = normal_values(arg_keys[5], (TILE_D, SLIDE_D), TILE_D ** -0.5, 0.15625, ((0, 4),))
    slide_gain = jnp.clip(1.0 + 0.15 * jax.random.normal(arg_keys[6], (SLIDE_D,), jnp.float32), 0.25, 1.75)
    w_qkv = draw_w_qkv(jax.random.fold_in(arg_keys[12], 71), 0)
    w_out = normal_values(arg_keys[8], (SLIDE_D, SLIDE_D), SLIDE_D ** -0.5, 0.21875, ((0, 4),))
    lengths = jax.vmap(lambda own: uneven(own, SLIDES, SEQ, 3 * SEQ // 4, 2))(jax.random.split(arg_keys[9], PACKS)).reshape((PACKS, SLIDES)).astype(jnp.int32)
    seg_len = plant(jax.random.randint(arg_keys[10], (HEADS,), TOK_DEV, SEQ + 1), jax.random.fold_in(arg_keys[10], 1), TOK_DEV, SEQ).astype(jnp.int32)
    rate = plant(jax.random.randint(arg_keys[11], (HEADS,), 1, 5), jax.random.fold_in(arg_keys[11], 1), 1, 4).astype(jnp.int32)
    return {"tile_feats": tile_feats, "tile_gain": tile_gain, "w_gate": w_gate, "w_up": w_up, "w_down": w_down, "w_proj": w_proj, "slide_gain": slide_gain, "w_qkv": w_qkv, "w_out": w_out, "lengths": lengths, "seg_len": seg_len, "rate": rate}


def layer_norm(rows, gain):
    mean = lax.optimization_barrier(jnp.mean(rows, axis=-1, keepdims=True))
    centered = rows - mean
    var = lax.optimization_barrier(jnp.mean(centered * centered, axis=-1, keepdims=True))
    return centered * lax.rsqrt(var + 1e-06) * gain

def slide_place(lengths_row, index):
    ends = jnp.cumsum(lengths_row, dtype=jnp.int32)
    after = index[:, None] >= ends[None, :]
    slide = lax.optimization_barrier(jnp.sum(after.astype(jnp.int32), axis=1, dtype=jnp.int32))
    before = lax.optimization_barrier(jnp.sum(jnp.where(after, lengths_row[None, :], 0), axis=1, dtype=jnp.int32))
    return (slide, index - before)

def allowed(q_slide, q_pos, q_idx, k_slide, k_pos, k_idx, seg, rate, heads):
    width = seg[:, None, None]
    step = rate[:, None, None]
    offset = (heads % rate)[:, None, None]
    same = (q_slide[:, None] == k_slide[None, :])[None]
    block = q_pos[None, :, None] // width == k_pos[None, None, :] // width
    pick = (k_pos[None, None, :] % step == offset) | (q_idx[:, None] == k_idx[None, :])[None]
    return same & block & pick

def pack_attention(query, key, value, lengths_row, seg_len, rate):
    index = jnp.arange(SEQ, dtype=jnp.int32)
    slide, pos = slide_place(lengths_row, index)
    heads = jnp.arange(HEADS, dtype=jnp.int32)
    qb = math.gcd(SEQ, 512)
    keys = key.reshape(SEQ, HEADS, HEAD_DIM).astype(jnp.float32)
    values = value.reshape(SEQ, HEADS, HEAD_DIM).astype(jnp.float32)
    scale = 1.0 / math.sqrt(HEAD_DIM)

    def one_block(number):
        start = (number * qb).astype(jnp.int32)
        rows = lax.dynamic_slice_in_dim(query, start, qb, 0).reshape(qb, HEADS, HEAD_DIM).astype(jnp.float32)
        q_idx = lax.dynamic_slice_in_dim(index, start, qb, 0)
        q_slide = lax.dynamic_slice_in_dim(slide, start, qb, 0)
        q_pos = lax.dynamic_slice_in_dim(pos, start, qb, 0)
        mask = allowed(q_slide, q_pos, q_idx, slide, pos, index, seg_len, rate, heads)
        scores = jnp.einsum('qhd,khd->hqk', rows, keys) * scale
        scores = jnp.where(mask, scores, -1e+30)
        top = lax.optimization_barrier(jnp.max(scores, axis=-1, keepdims=True))
        weights = jnp.where(mask, jnp.exp(scores - top), 0.0)
        weights = weights / lax.optimization_barrier(jnp.sum(weights, axis=-1, keepdims=True))
        out = jnp.einsum('hqk,khd->qhd', weights, values)
        return out.reshape(qb, SLIDE_D).astype(jnp.bfloat16)
    blocks = lax.map(one_block, jnp.arange(SEQ // qb, dtype=jnp.int32))
    return blocks.reshape(SEQ, SLIDE_D)

def reference(tile_feats, tile_gain, w_gate, w_up, w_down, w_proj, slide_gain, w_qkv, w_out, lengths, seg_len, rate):
    rows = tile_feats.reshape(PACKS * SEQ, TILE_D)
    normed = layer_norm(rows.astype(jnp.float32), tile_gain).astype(jnp.bfloat16)
    gate = jnp.dot(normed, w_gate, preferred_element_type=jnp.float32)
    up = jnp.dot(normed, w_up, preferred_element_type=jnp.float32)
    hidden = (jax.nn.silu(gate) * up).astype(jnp.bfloat16)
    tile_out = (rows.astype(jnp.float32) + jnp.dot(hidden, w_down, preferred_element_type=jnp.float32)).astype(jnp.bfloat16)
    emb = jnp.dot(tile_out, w_proj, preferred_element_type=jnp.float32)
    slide_normed = layer_norm(emb, slide_gain).astype(jnp.bfloat16)
    query = jnp.dot(slide_normed, w_qkv[0], preferred_element_type=jnp.float32).astype(jnp.bfloat16)
    key = jnp.dot(slide_normed, w_qkv[1], preferred_element_type=jnp.float32).astype(jnp.bfloat16)
    value = jnp.dot(slide_normed, w_qkv[2], preferred_element_type=jnp.float32).astype(jnp.bfloat16)
    outputs = []
    for pack in range(PACKS):
        lo = pack * SEQ
        outputs.append(pack_attention(query[lo:lo + SEQ], key[lo:lo + SEQ], value[lo:lo + SEQ], lengths[pack], seg_len, rate))
    att = jnp.concatenate(outputs, axis=0)
    slide_out = emb + jnp.dot(att, w_out, preferred_element_type=jnp.float32)
    return slide_out.astype(jnp.bfloat16).reshape(PACKS, SEQ, SLIDE_D)
```

```python
import functools
import math

import jax
import jax.numpy as jnp
from jax import lax
from jax.experimental import pallas as pl
from jax.experimental.pallas import tpu as pltpu
from jax.sharding import PartitionSpec as P

MESH = pl.DeviceIdType.MESH
BF = jnp.bfloat16
F32 = jnp.float32
NZ = 8
NY = 4
ROWS = 24
BLK = 128
HD = 48
NEG = -1e30
ANY = pl.BlockSpec(memory_space=pl.ANY)
VM = pl.BlockSpec(memory_space=pltpu.VMEM)


def rem(a, n):
    return lax.rem(a, jnp.int32(n))


def div(a, n):
    return lax.div(a, jnp.int32(n))


class Place:
    def __init__(self):
        self.s = lax.axis_index("section")
        self.q = lax.axis_index("seq")
        self.y = lax.axis_index("dp")
        self.xl = div(self.s, 2)
        self.c = rem(self.s, 2)
        self.xh = div(self.q, NZ)
        self.z = rem(self.q, NZ)
        self.x = self.xh * 2 + self.xl

    def at(self, xh=None, xl=None, c=None, z=None, y=None):
        xh = self.xh if xh is None else xh
        xl = self.xl if xl is None else xl
        c = self.c if c is None else c
        z = self.z if z is None else z
        y = self.y if y is None else y
        return {"section": xl * 2 + c, "seq": xh * NZ + z, "dp": y}

    def zat(self, d):
        return self.at(z=rem(self.z + d + NZ, NZ))

    def yat(self, d):
        return self.at(y=rem(self.y + d + NY, NY))

    def xpos(self, d):
        x = rem(self.x + d + 4, 4)
        return div(x, 2), rem(x, 2)

    def xat(self, d, c=None):
        xh, xl = self.xpos(d)
        return self.at(xh=xh, xl=xl, c=c)


def greet(devices):
    barrier = pltpu.get_barrier_semaphore()
    for device in devices:
        pl.semaphore_signal(barrier, inc=1, device_id=device, device_id_type=MESH)
    pl.semaphore_wait(barrier, len(devices))


class Link:
    def __init__(self, send_sem, recv_sem, local_sem=None):
        self.send_sem, self.recv_sem, self.local_sem = send_sem, recv_sem, local_sem
        self.sent = []
        self.local = 0

    def remote(self, src, dst, device):
        n = len(self.sent)
        copy = pltpu.make_async_remote_copy(
            src_ref=src,
            dst_ref=dst,
            send_sem=self.send_sem.at[n],
            recv_sem=self.recv_sem.at[n],
            device_id=device,
            device_id_type=MESH,
        )
        copy.start()
        self.sent.append(copy)
        return copy

    def here(self, src, dst):
        copy = pltpu.make_async_copy(src, dst, self.local_sem.at[self.local])
        self.local += 1
        copy.start()
        return copy

    def finish(self):
        for copy in self.sent:
            copy.wait_send()


def gather_kernel(
    wa, wb, mine, wp, wq, wo, wi, ga, gb, xs, gp, gq, go, gi, send_sem, recv_sem, local_sem
):
    me = Place()
    xh, xl, c, y, z, s = me.xh, me.xl, me.c, me.y, me.z, me.s
    other = 1 - c
    partner = me.at(c=other)
    across = me.at(xh=1 - xh)
    yp, ym, zp, zm = me.yat(1), me.yat(-1), me.zat(1), me.zat(-1)
    greet(
        [yp, ym, zp, zm, partner, across]
        + [me.xat(1), me.xat(1, other), me.xat(-1), me.xat(-1, other)]
    )
    link = Link(send_sem, recv_sem, local_sem)
    la = pl.ds(pl.multiple_of(c * 512, 512), 512)
    lb = pl.ds(pl.multiple_of(c * 1024, 1024), 1024)

    def yi(d):
        return rem(y + d + NY, NY)

    def zi(d):
        return rem(z + d + NZ, NZ)

    ex = [
        link.remote(wa.at[1 - xh], ga.at[xh, z, y, :, la], across),
        link.remote(wb.at[1 - xh], gb.at[xh, z, y, :, lb], across),
    ]
    lo = [
        link.here(wa.at[xh], ga.at[xh, z, y, :, la]),
        link.here(wb.at[xh], gb.at[xh, z, y, :, lb]),
    ]
    def feat(sec):
        return pl.ds(pl.multiple_of(sec * 384, 128), 384)

    x_direct = {}
    for d in (1, -1):
        for k in (0, 1):
            core = c if k == 0 else other
            x_direct[d, k] = link.remote(
                mine.at[:, core], xs.at[xh, :, :, feat(s)], me.xat(d, core)
            )
    x_pair = link.remote(mine.at[:, other], xs.at[xh, :, :, feat(s)], partner)
    x_own = link.here(mine.at[:, c], xs.at[xh, :, :, feat(s)])
    small = []
    for w, g in ((wi, gi), (wp, gp), (wq, gq), (wo, go)):
        half = w.shape[0] // 2
        up = link.remote(w.at[pl.ds(0, half)], g.at[s, pl.ds(0, half)], me.xat(1))
        dn = link.remote(w.at[pl.ds(half, half)], g.at[s, pl.ds(half, half)], me.xat(-1))
        own = link.remote(w, g.at[s], partner)
        small.append((g, up, dn, own, link.here(w, g.at[s])))

    for copy in ex:
        copy.wait_recv()
    for copy in lo:
        copy.wait()

    def gate_y(dst, yy, part=None):
        ref = ga.at[:, z, yy, :, la] if part is None else ga.at[part, z, yy, :, la]
        return link.remote(ref, ref, dst)

    def gate_z(dst, zz, part=None):
        ref = ga.at[:, zz, :, :, la] if part is None else ga.at[part, zz, :, :, la]
        return link.remote(ref, ref, dst)

    def rest(dst, zz, yy, part=None):
        ref = gb.at[:, zz, yy, :, lb] if part is None else gb.at[part, zz, yy, :, lb]
        return link.remote(ref, ref, dst)

    def pair_a(zz):
        ref = ga.at[:, zz, :, :, la]
        return link.remote(ref, ref, partner)

    def pair_b(zz):
        ref = gb.at[:, zz, :, :, lb]
        return link.remote(ref, ref, partner)

    pairs = []
    ay = {1: gate_y(yp, y), -1: gate_y(ym, y)}
    bz = {1: rest(zp, z, y), -1: rest(zm, z, y)}
    by, byo = {}, {}

    def spread(d):
        by[d] = (rest(yp, zi(d), y), rest(ym, zi(d), y))

    def pass_on(d):
        zz = zi(d)
        by[d][0].wait_recv()
        by[d][1].wait_recv()
        byo[d] = (rest(yp, zz, yi(-1), 0), rest(ym, zz, yi(1), 1))

    spread(0)
    ay[1].wait_recv()
    ay[-1].wait_recv()
    ayo = (gate_y(yp, yi(-1), 0), gate_y(ym, yi(1), 1))

    def hop_b(step):
        bz[1].wait_recv()
        bz[-1].wait_recv()
        part = (None, None) if step < 3 else (0, 1)
        if step < 4:
            bz[1] = rest(zp, zi(-step), y, part[0])
            bz[-1] = rest(zm, zi(step), y, part[1])
        spread(-step)
        if step < 4:
            spread(step)

    hop_b(1)
    ayo[0].wait_recv()
    ayo[1].wait_recv()
    az = {1: gate_z(zp, z), -1: gate_z(zm, z)}
    pairs.append(pair_a(z))

    def hop_a(step):
        az[1].wait_recv()
        az[-1].wait_recv()
        part = (None, None) if step < 3 else (0, 1)
        if step < 4:
            az[1] = gate_z(zp, zi(-step), part[0])
            az[-1] = gate_z(zm, zi(step), part[1])
        pairs.append(pair_a(zi(-step)))
        if step < 4:
            pairs.append(pair_a(zi(step)))

    pass_on(0)
    x_far = []
    for d in (1, -1):
        xxh, xxl = me.xpos(-d)
        row = 0 if d == 1 else 1
        for k in (0, 1):
            x_direct[d, k].wait_recv()
            sec = xxl * 2 + (c if k == 0 else other)
            ref = xs.at[xxh, row, :, feat(sec)]
            x_far.append(link.remote(ref, ref, me.xat(d)))
    hop_b(2)
    pass_on(-1)
    pass_on(1)
    hop_a(1)
    hop_b(3)
    pass_on(-2)
    pass_on(2)
    hop_a(2)
    hop_b(4)
    pass_on(-3)
    pass_on(3)
    hop_a(3)
    pass_on(-4)

    def whole(d):
        byo[d][0].wait_recv()
        byo[d][1].wait_recv()
        pairs.append(pair_b(zi(d)))

    for d in (0, -1, 1, -2, 2):
        whole(d)
    hop_a(4)
    for d in (-3, 3, -4):
        whole(d)
    far = (1 - xl) * 2 + c
    for g, up, dn, own, local in small:
        up.wait_recv()
        dn.wait_recv()
        pairs.append(link.remote(g.at[far], g.at[far], partner))
    for g, up, dn, own, local in small:
        own.wait_recv()
        local.wait()
    x_pair.wait_recv()
    x_own.wait()
    for copy in x_far + pairs:
        copy.wait_recv()
    link.finish()


def scatter_kernel(t, r, stage, send_sem, recv_sem):
    me = Place()
    xp, xm = me.xat(1), me.xat(-1)
    greet([xp, xm])
    link = Link(send_sem, recv_sem)
    h = BLK // 2

    def part(d):
        return me.xpos(d)

    oh, ol = part(2)
    first = link.remote(t.at[oh, ol, pl.ds(0, h)], stage.at[0], xp)
    second = link.remote(t.at[oh, ol, pl.ds(h, h)], stage.at[1], xm)
    ph, pw = part(1)
    mh, mw = part(-1)
    a = link.remote(t.at[ph, pw], r.at[0], xp)
    b = link.remote(t.at[mh, mw], r.at[1], xm)
    first.wait_recv()
    far0 = link.remote(stage.at[0], r.at[2, pl.ds(0, h)], xp)
    second.wait_recv()
    far1 = link.remote(stage.at[1], r.at[2, pl.ds(h, h)], xm)
    for copy in (a, b, far0, far1):
        copy.wait_recv()
    link.finish()


NEAR = (1, 7, 2, 6, 3, 5, 4)


def heads_kernel(qkv, f, stage, send_sem, recv_sem, local_sem):
    me = Place()
    xh, xl, c, z = me.xh, me.xl, me.c, me.z
    flip = me.at(xl=1 - xl)
    cross = me.at(xh=1 - xh, xl=1 - xl)
    partner = me.at(c=1 - c)
    greet([me.zat(d) for d in range(1, NZ)] + [flip, cross, partner])
    link = Link(send_sem, recv_sem, local_sem)
    kv = pl.ds(0, 2 * HD)

    def zi(d):
        return rem(z + d + NZ, NZ)

    keep, move = {}, {}
    own = link.here(qkv.at[z * 2 + xh], f.at[xh, z, xl, c])
    for d in NEAR:
        zz = zi(d)
        keep[d] = link.remote(qkv.at[zz * 2 + xh], f.at[xh, z, xl, c], me.zat(d))
        move[d] = link.remote(qkv.at[zz * 2 + 1 - xh], stage.at[z], me.zat(d))
    to_cross = {0: link.remote(qkv.at[z * 2 + 1 - xh], f.at[xh, z, xl, c], cross)}
    to_flip = {0: link.remote(qkv.at[z * 2 + xh, kv], f.at[xh, z, xl, c, kv], flip)}
    relay = {}

    def pass_on(d):
        to_cross[d].wait_recv()
        ref = f.at[1 - xh, zi(-d), 1 - xl, c]
        relay[d] = link.remote(ref, ref, flip)

    last = None
    for d in NEAR:
        zz = zi(-d)
        move[d].wait_recv()
        to_cross[d] = link.remote(stage.at[zz], f.at[xh, zz, xl, c], cross)
        keep[d].wait_recv()
        ref = f.at[xh, zz, xl, c, kv]
        to_flip[d] = link.remote(ref, ref, flip)
        if last is not None:
            pass_on(last)
        last = d if last is not None else 0
        if d == NEAR[1]:
            pass_on(NEAR[0])
            last = d
    pass_on(last)
    own.wait()
    pairs = []

    def pair(xxh, xxl):
        ref = f.at[xxh, :, xxl, c, kv]
        pairs.append(link.remote(ref, ref, partner))

    pair(xh, xl)
    for d in range(NZ):
        to_flip[d].wait_recv()
    pair(xh, 1 - xl)
    pair(1 - xh, 1 - xl)
    for d in range(NZ):
        relay[d].wait_recv()
    pair(1 - xh, xl)
    for copy in pairs:
        copy.wait_recv()
    link.finish()


def back_kernel(o, a, send_sem, recv_sem, local_sem):
    me = Place()
    xh, z = me.xh, me.z
    places = [(e, d) for e in (0, 1) for d in range(NZ) if (e, d) != (0, 0)]

    def target(e, d):
        zz = rem(z + d, NZ)
        xx = xh if e == 0 else 1 - xh
        return xx, zz

    devices = []
    for e, d in places:
        xx, zz = target(e, d)
        devices.append(me.at(xh=xx, z=zz))
    greet(devices)
    link = Link(send_sem, recv_sem, local_sem)
    head = z * 2 + xh
    for (e, d), device in zip(places, devices):
        xx, zz = target(e, d)
        link.remote(o.at[xx * NZ + zz], a.at[head], device)
    own = link.here(o.at[xh * NZ + z], a.at[head])
    for copy in list(link.sent):
        copy.wait_recv()
    own.wait()
    link.finish()


def out_kernel(o, full, send_sem, recv_sem, local_sem):
    me = Place()
    xl, c, s = me.xl, me.c, me.s
    spots = [(xl, 1 - c), (1 - xl, c), (1 - xl, 1 - c)]
    greet([me.at(xl=a, c=b) for a, b in spots])
    link = Link(send_sem, recv_sem, local_sem)
    for a, b in spots:
        link.remote(o.at[a * 2 + b], full.at[s], me.at(xl=a, c=b))
    own = link.here(o.at[s], full.at[s])
    for copy in list(link.sent):
        copy.wait_recv()
    own.wait()
    link.finish()


QT = 256
KT = 512
KB = KT // BLK


def attention_kernel(lo_ref, hi_ref, f_ref, kid_ref, qid_ref, free_ref, o_ref, k_s, v_s, id_s):
    t = pl.program_id(0)
    s = lax.axis_index("section")
    blocks = f_ref.shape[0]
    factor = math.log2(math.e) / math.sqrt(HD)

    @pl.when(t == 0)
    def _():
        v_s[:, HD:, :] = jnp.ones_like(v_s[:, HD:, :])

        def prep(n, carry):
            for j in range(KB):
                b = n * KB + j
                k_s[b] = f_ref[b, :HD].astype(F32).T.astype(BF)
                v_s[n, :HD, j * BLK : (j + 1) * BLK] = f_ref[b, HD : 2 * HD]
                ids = jnp.broadcast_to(kid_ref[pl.ds(b, 1), :], (BLK, BLK))
                id_s[b] = ids.T
            return carry

        lax.fori_loop(0, blocks // KB, prep, 0)

    parts = [f_ref[(t * 2 + j) * 4 + s] for j in range(2)]
    own = jnp.concatenate(parts, axis=1)
    query = own[2 * HD :]
    qid = qid_ref[pl.ds(t, 1), :]
    free = free_ref[pl.ds(t, 1), :]
    top = jnp.sum(query.astype(F32) * own[:HD].astype(F32), axis=0, keepdims=True)
    acc = jnp.concatenate(
        [own[HD : 2 * HD].astype(F32) * free, jnp.broadcast_to(free, (v_s.shape[1] - HD, QT))], axis=0
    )

    def body(n, carry):
        top, acc = carry
        keys = k_s[pl.ds(n * KB, KB)].reshape(KT, HD)
        scores = jnp.dot(keys, query, preferred_element_type=F32)
        ids = id_s[pl.ds(n * KB, KB)].reshape(KT, BLK)
        ids = jnp.concatenate([ids, ids], axis=1)
        scores = jnp.where(ids == qid, scores, NEG)
        fresh = jnp.maximum(top, jnp.max(scores, axis=0, keepdims=True))
        weights = jnp.exp2((scores - fresh) * factor)
        acc = acc * jnp.exp2((top - fresh) * factor) + jnp.dot(
            v_s[n], weights.astype(BF), preferred_element_type=F32
        )
        return fresh, acc

    top, acc = lax.fori_loop(lo_ref[t], hi_ref[t], body, (top, acc))
    result = (acc[:HD] / acc[HD : HD + 1]).astype(BF)
    for j in range(2):
        o_ref[j] = result[:, j * BLK : (j + 1) * BLK]


def sems(n):
    return [pltpu.SemaphoreType.DMA((n,)), pltpu.SemaphoreType.DMA((n,))]


def comm(kernel, ident, outs, copies, local, scratch, *args):
    extra = list(scratch) + sems(copies)
    if local:
        extra.append(pltpu.SemaphoreType.DMA((local,)))
    return pl.pallas_call(
        kernel,
        out_shape=[jax.ShapeDtypeStruct(shape, kind) for shape, kind in outs],
        in_specs=[ANY] * len(args),
        out_specs=[ANY] * len(outs),
        scratch_shapes=extra,
        compiler_params=pltpu.CompilerParams(collective_id=ident, has_side_effects=True),
    )(*args)


def layer_norm(rows, gain):
    mean = jnp.mean(rows, axis=-1, keepdims=True)
    centered = rows - mean
    var = jnp.mean(centered * centered, axis=-1, keepdims=True)
    return centered * lax.rsqrt(var + 1e-06) * gain


def dot(a, b, dims):
    return lax.dot_general(a, b, (dims, ((), ())), preferred_element_type=F32)


def attention(f, lengths_row, seg_len, rate, head):
    total = 64 * BLK
    index = jnp.arange(total, dtype=jnp.int32)
    ends = jnp.cumsum(lengths_row, dtype=jnp.int32)
    after = index[:, None] >= ends[None, :]
    slide = jnp.sum(after.astype(jnp.int32), axis=1, dtype=jnp.int32)
    start = jnp.sum(jnp.where(after, lengths_row[None, :], 0), axis=1, dtype=jnp.int32)
    size = jnp.sum(
        jnp.where(slide[:, None] == jnp.arange(3)[None, :], lengths_row[None, :], 0), axis=1
    )
    pos = index - start
    segment = pos // seg_len
    ident = slide * 16384 + segment
    picked = pos % rate == head % rate
    kid = jnp.where(picked, ident, -1).astype(F32).reshape(64, BLK)
    begin = start + segment * seg_len
    end = start + jnp.minimum(size, (segment + 1) * seg_len)
    section = lax.axis_index("section")

    def of_queries(values):
        values = values.reshape(16, 4, BLK)
        return lax.dynamic_index_in_dim(values, section, 1, keepdims=False).reshape(8, QT)

    qid = of_queries(ident).astype(F32)
    free = of_queries(1.0 - picked.astype(F32))
    lo = jnp.min(of_queries(begin), axis=1) // KT
    hi = (jnp.max(of_queries(end), axis=1) + KT - 1) // KT
    spec = pltpu.PrefetchScalarGridSpec(
        num_scalar_prefetch=2,
        grid=(8,),
        in_specs=[
            pl.BlockSpec((64, 3 * HD, BLK), lambda t, lo, hi: (0, 0, 0)),
            pl.BlockSpec((64, BLK), lambda t, lo, hi: (0, 0)),
            pl.BlockSpec((8, QT), lambda t, lo, hi: (0, 0)),
            pl.BlockSpec((8, QT), lambda t, lo, hi: (0, 0)),
        ],
        out_specs=pl.BlockSpec((2, HD, BLK), lambda t, lo, hi: (t, 0, 0)),
        scratch_shapes=[
            pltpu.VMEM((64, BLK, HD), BF),
            pltpu.VMEM((16, 64, KT), BF),
            pltpu.VMEM((64, BLK, BLK), F32),
        ],
    )
    return pl.pallas_call(
        attention_kernel,
        grid_spec=spec,
        out_shape=jax.ShapeDtypeStruct((16, HD, BLK), BF),
        compiler_params=pltpu.CompilerParams(dimension_semantics=("arbitrary",)),
    )(lo, hi, f.reshape(64, 3 * HD, BLK), kid, qid, free)


def per_device(
    tile_feats,
    tile_gain,
    w_gate,
    w_up,
    w_down,
    w_proj,
    slide_gain,
    w_qkv,
    w_out,
    lengths,
    seg_len,
    rate,
):
    section = lax.axis_index("section")
    seq = lax.axis_index("seq")
    xh, z = seq // NZ, seq % NZ
    xl = section // 2

    def halves(w):
        return w.reshape(ROWS, 2, 512).transpose(1, 0, 2)

    wa = halves(w_gate)
    wb = jnp.concatenate([halves(w_up), halves(w_down.T)], axis=2)
    wq = jnp.stack([w_qkv[1], w_qkv[2], w_qkv[0]]).reshape(3, 768, 4, HD)
    wq = wq.transpose(2, 0, 3, 1).reshape(576, 768)
    mine = tile_feats[0].reshape(2, 2, BLK, 384)
    wi = jnp.concatenate([seg_len, rate]).reshape(8, 1)
    wi = jnp.broadcast_to(jnp.pad(wi, ((0, 8), (0, 0))), (16, BLK))
    ga, gb, xs, gp, gq, go, gi = comm(
        gather_kernel,
        0,
        [
            ((2, NZ, NY, ROWS, 1024), BF),
            ((2, NZ, NY, ROWS, 2048), BF),
            ((2, 2, BLK, 1536), BF),
            ((4, 384, 768), BF),
            ((4, 576, 768), BF),
            ((4, 192, 768), BF),
            ((4, 16, BLK), jnp.int32),
        ],
        120,
        8,
        [],
        wa,
        wb,
        mine,
        w_proj,
        wq,
        w_out,
        wi,
    )
    rows = xs.reshape(4 * BLK, 1536)
    normed = layer_norm(rows.astype(F32), tile_gain).astype(BF)
    ga = ga.reshape(1536, 1024)
    gb = gb.reshape(1536, 2048)
    gate = dot(normed, ga, ((1,), (0,)))
    part = None
    for core in range(2):
        up = dot(normed, gb[:, core * 1024 : core * 1024 + 512], ((1,), (0,)))
        hidden = (jax.nn.silu(gate[:, core * 512 : core * 512 + 512]) * up).astype(BF)
        term = dot(hidden, gb[:, core * 1024 + 512 : core * 1024 + 1024], ((1,), (1,)))
        part = term if part is None else part + term
    part = part.astype(BF).reshape(2, 2, BLK, 1536)
    (others,) = comm(
        scatter_kernel,
        1,
        [((3, BLK, 1536), BF)],
        8,
        0,
        [pltpu.VMEM((2, BLK // 2, 1536), BF)],
        part,
    )
    own = part[xh, xl].astype(F32) + jnp.sum(others.astype(F32), axis=0)
    tile_out = (xs[xh, xl].astype(F32) + own).astype(BF)
    emb = dot(tile_out, gp.reshape(1536, 768), ((1,), (0,)))
    slide_normed = layer_norm(emb, slide_gain).astype(BF)
    qkv = dot(gq.reshape(2304, 768), slide_normed, ((1,), (1,))).astype(BF)
    (f,) = comm(
        heads_kernel,
        2,
        [((2, NZ, 2, 2, 3 * HD, BLK), BF)],
        50,
        1,
        [pltpu.VMEM((NZ, 3 * HD, BLK), BF)],
        qkv.reshape(16, 3 * HD, BLK),
    )
    head = z * 2 + xh
    segs = gi[:, :4, 0].reshape(16)
    rates = gi[:, 4:8, 0].reshape(16)
    o = attention(f, lengths[0], segs[head], rates[head], head)
    (att,) = comm(back_kernel, 3, [((16, HD, BLK), BF)], 16, 1, [], o)
    out = emb + dot(att.reshape(768, BLK), go.reshape(768, 768), ((0,), (0,)))
    out = out.astype(BF).reshape(BLK, 4, 192).transpose(1, 0, 2)
    (full,) = comm(out_kernel, 4, [((4, BLK, 192), BF)], 4, 1, [], out)
    return full.reshape(1, 4 * BLK, 192)


def solution(mesh):
    placed = (
        P("dp", "seq", "section"),
        P(),
        P(("seq", "dp"), "section"),
        P(("seq", "dp"), "section"),
        P("section", ("seq", "dp")),
        P("section", None),
        P(),
        P(None, None, "section"),
        P("section", None),
        P("dp", None),
        P("section"),
        P("section"),
    )
    return jax.shard_map(
        per_device, mesh=mesh, in_specs=placed, out_specs=P("dp", "seq", "section"), check_vma=False
    )
```

```python
import functools
import math

import jax
import jax.numpy as jnp
from jax import lax
from jax.experimental import pallas as pl
from jax.experimental.pallas import tpu as pltpu
from jax.sharding import PartitionSpec as P

MESH = pl.DeviceIdType.MESH
BF = jnp.bfloat16
F32 = jnp.float32
NZ = 8
NY = 4
ROWS = 24
BLK = 128
HD = 48
NEG = -(2.0**100)
SEGS = 32
ANY = pl.BlockSpec(memory_space=pl.ANY)
VM = pl.BlockSpec(memory_space=pltpu.VMEM)


def rem(a, n):
    return lax.rem(a, jnp.int32(n))


def div(a, n):
    return lax.div(a, jnp.int32(n))


class Place:
    def __init__(self):
        self.s = lax.axis_index("section")
        self.q = lax.axis_index("seq")
        self.y = lax.axis_index("dp")
        self.xl = div(self.s, 2)
        self.c = rem(self.s, 2)
        self.xh = div(self.q, NZ)
        self.z = rem(self.q, NZ)
        self.x = self.xh * 2 + self.xl

    def at(self, xh=None, xl=None, c=None, z=None, y=None):
        xh = self.xh if xh is None else xh
        xl = self.xl if xl is None else xl
        c = self.c if c is None else c
        z = self.z if z is None else z
        y = self.y if y is None else y
        return {"section": xl * 2 + c, "seq": xh * NZ + z, "dp": y}

    def zat(self, d):
        return self.at(z=rem(self.z + d + NZ, NZ))

    def yat(self, d):
        return self.at(y=rem(self.y + d + NY, NY))

    def xpos(self, d):
        x = rem(self.x + d + 4, 4)
        return div(x, 2), rem(x, 2)

    def xat(self, d, c=None):
        xh, xl = self.xpos(d)
        return self.at(xh=xh, xl=xl, c=c)


def greet(devices):
    barrier = pltpu.get_barrier_semaphore()
    for device in devices:
        pl.semaphore_signal(barrier, inc=1, device_id=device, device_id_type=MESH)
    pl.semaphore_wait(barrier, len(devices))


class Link:
    def __init__(self, send_sem, recv_sem, local_sem=None):
        self.send_sem, self.recv_sem, self.local_sem = send_sem, recv_sem, local_sem
        self.sent = []
        self.local = 0

    def remote(self, src, dst, device):
        n = len(self.sent)
        copy = pltpu.make_async_remote_copy(
            src_ref=src,
            dst_ref=dst,
            send_sem=self.send_sem.at[n],
            recv_sem=self.recv_sem.at[n],
            device_id=device,
            device_id_type=MESH,
        )
        copy.start()
        self.sent.append(copy)
        return copy

    def here(self, src, dst):
        copy = pltpu.make_async_copy(src, dst, self.local_sem.at[self.local])
        self.local += 1
        copy.start()
        return copy

    def finish(self):
        for copy in self.sent:
            copy.wait_send()


def gather_kernel(
    wg, wu, wd, mine, wp, wq, wo, wi, ga, gb, xs, gp, gq, go, gi,
    vw, vx, vp, vq, vo, vi, send_sem, recv_sem, local_sem
):
    me = Place()
    xh, xl, c, y, z, s = me.xh, me.xl, me.c, me.y, me.z, me.s
    other = 1 - c
    partner = me.at(c=other)
    across = me.at(xh=1 - xh)
    yp, ym, zp, zm = me.yat(1), me.yat(-1), me.zat(1), me.zat(-1)
    greet(
        [yp, ym, zp, zm, partner, across]
        + [me.xat(1), me.xat(1, other), me.xat(-1), me.xat(-1, other)]
    )
    link = Link(send_sem, recv_sem, local_sem)
    la = pl.ds(pl.multiple_of(c * 512, 512), 512)
    lb = pl.ds(pl.multiple_of(c * 1024, 1024), 1024)

    def yi(d):
        return rem(y + d + NY, NY)

    def zi(d):
        return rem(z + d + NZ, NZ)

    ex, lo = [], []

    def cols(half):
        return pl.ds(pl.multiple_of(half * 512, 512), 512)

    for n, (w, g, first) in enumerate(
        ((wg, ga, c * 512), (wu, gb, c * 1024), (wd, gb, c * 1024 + 512))
    ):
        spot = g.at[xh, z, y, :, pl.ds(pl.multiple_of(first, 512), 512)]
        ex.append(link.remote(w.at[:, cols(1 - xh)], spot, across))
        lo.append((link.here(w.at[:, cols(xh)], vw.at[n]), vw.at[n], spot))
    def feat(sec):
        return pl.ds(pl.multiple_of(sec * 384, 128), 384)

    x_direct = {}
    for d in (1, -1):
        for k in (0, 1):
            core = c if k == 0 else other
            x_direct[d, k] = link.remote(
                mine.at[:, core], xs.at[xh, :, :, feat(s)], me.xat(d, core)
            )
    x_pair = link.remote(mine.at[:, other], xs.at[xh, :, :, feat(s)], partner)
    x_in = link.here(mine.at[:, c], vx)
    small = ((wi, gi, vi), (wp, gp, vp), (wq, gq, vq), (wo, go, vo))
    small_in = [link.here(w, v) for w, g, v in small]
    lo_out = []
    for copy, via, spot in lo:
        copy.wait()
        lo_out.append(link.here(via, spot))
    for copy in ex:
        copy.wait_recv()
    for copy in lo_out:
        copy.wait()
    x_in.wait()
    x_own = link.here(vx, xs.at[xh, :, :, feat(s)])

    def gate_y(dst, yy, part=None):
        ref = ga.at[:, z, yy, :, la] if part is None else ga.at[part, z, yy, :, la]
        return link.remote(ref, ref, dst)

    def gate_z(dst, zz, part=None):
        ref = ga.at[:, zz, :, :, la] if part is None else ga.at[part, zz, :, :, la]
        return link.remote(ref, ref, dst)

    def rest(dst, zz, yy, part=None):
        ref = gb.at[:, zz, yy, :, lb] if part is None else gb.at[part, zz, yy, :, lb]
        return link.remote(ref, ref, dst)

    def pair_a(zz):
        ref = ga.at[:, zz, :, :, la]
        return link.remote(ref, ref, partner)

    def pair_b(zz):
        ref = gb.at[:, zz, :, :, lb]
        return link.remote(ref, ref, partner)

    pairs = []
    ay = {1: gate_y(yp, y), -1: gate_y(ym, y)}
    bz = {1: rest(zp, z, y), -1: rest(zm, z, y)}
    by, byo = {}, {}

    def spread(d):
        by[d] = (rest(yp, zi(d), y), rest(ym, zi(d), y))

    def pass_on(d):
        zz = zi(d)
        by[d][0].wait_recv()
        by[d][1].wait_recv()
        byo[d] = (rest(yp, zz, yi(-1), 0), rest(ym, zz, yi(1), 1))

    spread(0)
    ay[1].wait_recv()
    ay[-1].wait_recv()
    ayo = (gate_y(yp, yi(-1), 0), gate_y(ym, yi(1), 1))

    def hop_b(step):
        bz[1].wait_recv()
        bz[-1].wait_recv()
        part = (None, None) if step < 3 else (0, 1)
        if step < 4:
            bz[1] = rest(zp, zi(-step), y, part[0])
            bz[-1] = rest(zm, zi(step), y, part[1])
        spread(-step)
        if step < 4:
            spread(step)

    hop_b(1)
    ayo[0].wait_recv()
    ayo[1].wait_recv()
    az = {(d, p): gate_z(zp if d == 1 else zm, z, p) for p in (0, 1) for d in (1, -1)}
    pairs.append(pair_a(z))

    def hop_a(step):
        for p in (0, 1):
            for d in (1, -1):
                if step < 4 or (d, p) in ((1, 0), (-1, 1)):
                    az[d, p].wait_recv()
                if step < 3 or (step == 3 and (d, p) in ((1, 0), (-1, 1))):
                    az[d, p] = gate_z(zp if d == 1 else zm, zi(-step * d), p)
        pairs.append(pair_a(zi(-step)))
        if step < 4:
            pairs.append(pair_a(zi(step)))

    pass_on(0)
    hop_b(2)
    x_far = []
    for d in (1, -1):
        xxh, xxl = me.xpos(-d)
        row = 0 if d == 1 else 1
        for k in (0, 1):
            x_direct[d, k].wait_recv()
            sec = xxl * 2 + (c if k == 0 else other)
            ref = xs.at[xxh, row, :, feat(sec)]
            x_far.append(link.remote(ref, ref, me.xat(d)))
    sent_small = []
    for (w, g, v), copy in zip(small, small_in):
        half = w.shape[0] // 2
        up = link.remote(w.at[pl.ds(0, half)], g.at[s, pl.ds(0, half)], me.xat(1))
        dn = link.remote(w.at[pl.ds(half, half)], g.at[s, pl.ds(half, half)], me.xat(-1))
        own = link.remote(w, g.at[s], partner)
        copy.wait()
        sent_small.append((g, up, dn, own, link.here(v, g.at[s])))

    pass_on(-1)
    pass_on(1)
    hop_a(1)
    hop_b(3)
    pass_on(-2)
    pass_on(2)
    hop_a(2)
    hop_b(4)

    def whole(d):
        byo[d][0].wait_recv()
        byo[d][1].wait_recv()
        pairs.append(pair_b(zi(d)))

    pass_on(-3)
    pass_on(3)
    whole(0)
    hop_a(3)
    pass_on(-4)
    for d in (-1, 1, -2, 2):
        whole(d)
    hop_a(4)
    far = (1 - xl) * 2 + c

    def whole_small(n):
        g, up, dn, own, local = sent_small[n]
        up.wait_recv()
        dn.wait_recv()
        pairs.append(link.remote(g.at[far], g.at[far], partner))

    whole_small(0)
    whole_small(1)
    for d in (-3, 3, -4):
        whole(d)
    whole_small(2)
    whole_small(3)
    for g, up, dn, own, local in sent_small:
        own.wait_recv()
        local.wait()
    x_pair.wait_recv()
    x_own.wait()
    for copy in x_far + pairs:
        copy.wait_recv()
    link.finish()


def scatter_kernel(t, r, stage, send_sem, recv_sem):
    me = Place()
    xp, xm = me.xat(1), me.xat(-1)
    greet([xp, xm])
    link = Link(send_sem, recv_sem)
    h = BLK // 2

    def part(d):
        return me.xpos(d)

    oh, ol = part(2)
    first = link.remote(t.at[oh, ol, pl.ds(0, h)], stage.at[0], xp)
    second = link.remote(t.at[oh, ol, pl.ds(h, h)], stage.at[1], xm)
    ph, pw = part(1)
    mh, mw = part(-1)
    a = link.remote(t.at[ph, pw], r.at[0], xp)
    b = link.remote(t.at[mh, mw], r.at[1], xm)
    first.wait_recv()
    far0 = link.remote(stage.at[0], r.at[2, pl.ds(0, h)], xp)
    second.wait_recv()
    far1 = link.remote(stage.at[1], r.at[2, pl.ds(h, h)], xm)
    for copy in (a, b, far0, far1):
        copy.wait_recv()
    link.finish()


NEAR = (1, 7, 2, 6, 3, 5, 4)


def heads_kernel(qkv, f, stage, send_sem, recv_sem, local_sem):
    me = Place()
    xh, xl, c, z = me.xh, me.xl, me.c, me.z
    flip = me.at(xl=1 - xl)
    cross = me.at(xh=1 - xh, xl=1 - xl)
    partner = me.at(c=1 - c)
    greet([me.zat(d) for d in range(1, NZ)] + [flip, cross, partner])
    link = Link(send_sem, recv_sem, local_sem)
    kv = pl.ds(1, 2)

    def head(zz, e):
        n = zz * 2 + e
        return qkv.at[div(n, 4), :, rem(n, 4)]

    def head_kv(zz, e):
        n = zz * 2 + e
        return qkv.at[div(n, 4), kv, rem(n, 4)]

    def zi(d):
        return rem(z + d + NZ, NZ)

    keep, move = {}, {}
    own = link.here(head(z, xh), f.at[xh, z, xl, c])
    for d in NEAR:
        zz = zi(d)
        keep[d] = link.remote(head(zz, xh), f.at[xh, z, xl, c], me.zat(d))
        move[d] = link.remote(head(zz, 1 - xh), stage.at[z], me.zat(d))
    to_cross = {0: link.remote(head(z, 1 - xh), f.at[xh, z, xl, c], cross)}
    to_flip = {0: link.remote(head_kv(z, xh), f.at[xh, z, xl, c, kv], flip)}
    relay = {}

    def pass_on(d):
        to_cross[d].wait_recv()
        ref = f.at[1 - xh, zi(-d), 1 - xl, c]
        relay[d] = link.remote(ref, ref, flip)

    last = None
    for d in NEAR:
        zz = zi(-d)
        move[d].wait_recv()
        to_cross[d] = link.remote(stage.at[zz], f.at[xh, zz, xl, c], cross)
        keep[d].wait_recv()
        ref = f.at[xh, zz, xl, c, kv]
        to_flip[d] = link.remote(ref, ref, flip)
        if last is not None:
            pass_on(last)
        last = d if last is not None else 0
        if d == NEAR[1]:
            pass_on(NEAR[0])
            last = d
    pass_on(last)
    own.wait()
    pairs = []

    def pair(xxh, xxl):
        ref = f.at[xxh, :, xxl, c, kv]
        pairs.append(link.remote(ref, ref, partner))

    pair(xh, xl)
    for d in range(NZ):
        to_flip[d].wait_recv()
    pair(xh, 1 - xl)
    pair(1 - xh, 1 - xl)
    for d in range(NZ):
        relay[d].wait_recv()
    pair(1 - xh, xl)
    for copy in pairs:
        copy.wait_recv()
    link.finish()


def back_kernel(o, a, send_sem, recv_sem, local_sem):
    me = Place()
    xh, z = me.xh, me.z
    places = [(e, d) for e in (0, 1) for d in range(NZ) if (e, d) != (0, 0)]

    def target(e, d):
        zz = rem(z + d, NZ)
        xx = xh if e == 0 else 1 - xh
        return xx, zz

    devices = []
    for e, d in places:
        xx, zz = target(e, d)
        devices.append(me.at(xh=xx, z=zz))
    greet(devices)
    link = Link(send_sem, recv_sem, local_sem)
    head = z * 2 + xh
    for (e, d), device in zip(places, devices):
        xx, zz = target(e, d)
        link.remote(o.at[xx * NZ + zz], a.at[head], device)
    own = link.here(o.at[xh * NZ + z], a.at[head])
    for copy in list(link.sent):
        copy.wait_recv()
    own.wait()
    link.finish()


def out_kernel(o, full, send_sem, recv_sem, local_sem):
    me = Place()
    xl, c, s = me.xl, me.c, me.s
    here = pl.ds(pl.multiple_of(s * BLK, BLK), BLK)
    spots = [(xl, 1 - c), (1 - xl, c), (1 - xl, 1 - c)]
    greet([me.at(xl=a, c=b) for a, b in spots])
    link = Link(send_sem, recv_sem, local_sem)
    for a, b in spots:
        link.remote(o.at[a * 2 + b], full.at[:, here], me.at(xl=a, c=b))
    own = link.here(o.at[s], full.at[:, here])
    for copy in list(link.sent):
        copy.wait_recv()
    own.wait()
    link.finish()


QT = 512
KT = 256
UNROLL = 4
KB = KT // BLK


def attention_kernel(lo_ref, hi_ref, f_ref, kmask_ref, hot_ref, free_ref, o_ref, k_s, v_s):
    t = pl.program_id(0)
    s = lax.axis_index("section")
    blocks = f_ref.shape[0]
    factor = math.log2(math.e) / math.sqrt(HD)

    @pl.when(t == 0)
    def _():
        v_s[:, HD:, :] = jnp.ones_like(v_s[:, HD:, :])

        def prep(n, carry):
            for j in range(KB):
                b = n * KB + j
                key = f_ref[b, 1]
                k_s[b] = jnp.concatenate([key, key, kmask_ref[b]], axis=0).T
                v_s[n, :HD, j * BLK : (j + 1) * BLK] = f_ref[b, 2]
            return carry

        lax.fori_loop(0, blocks // KB, prep, 0)

    def mine(part):
        each = QT // BLK
        return jnp.concatenate(
            [f_ref[(t * each + j) * 4 + s, part].astype(F32) for j in range(each)], axis=1
        )

    scaled = mine(0) * factor
    high = scaled.astype(BF)
    low = (scaled - high.astype(F32)).astype(BF)
    query = jnp.concatenate([high, low, hot_ref[0]], axis=0)
    free = free_ref[pl.ds(t, 1), :]
    top = jnp.sum(scaled * mine(1), axis=0, keepdims=True)
    acc = jnp.concatenate(
        [mine(2) * free, jnp.broadcast_to(free, (v_s.shape[1] - HD, QT))], axis=0
    )

    def body(m, carry):
        top, acc = carry
        scores = []
        for u in range(UNROLL):
            n = m * UNROLL + u
            keys = k_s[pl.ds(n * KB, KB)].reshape(KT, BLK)
            scores.append(jnp.dot(keys, query, preferred_element_type=F32))
        for u in range(UNROLL):
            n = m * UNROLL + u
            fresh = jnp.maximum(top, jnp.max(scores[u], axis=0, keepdims=True))
            weights = jnp.exp2(scores[u] - fresh)
            acc = acc * jnp.exp2(top - fresh) + jnp.dot(
                v_s[n], weights.astype(BF), preferred_element_type=F32
            )
            top = fresh
        return top, acc

    top, acc = lax.fori_loop(lo_ref[t], hi_ref[t], body, (top, acc))
    result = (acc[:HD] / acc[HD : HD + 1]).astype(BF)
    for j in range(QT // BLK):
        o_ref[j] = result[:, j * BLK : (j + 1) * BLK]


def sems(n):
    return [pltpu.SemaphoreType.DMA((n,)), pltpu.SemaphoreType.DMA((n,))]


def comm(kernel, ident, outs, copies, local, scratch, *args, place=ANY):
    extra = list(scratch) + sems(copies)
    if local:
        extra.append(pltpu.SemaphoreType.DMA((local,)))
    return pl.pallas_call(
        kernel,
        out_shape=[jax.ShapeDtypeStruct(shape, kind) for shape, kind in outs],
        in_specs=[place] * len(args),
        out_specs=[ANY] * len(outs),
        scratch_shapes=extra,
        compiler_params=pltpu.CompilerParams(collective_id=ident, has_side_effects=True),
    )(*args)


def layer_norm(rows, gain):
    mean = jnp.mean(rows, axis=-1, keepdims=True)
    centered = rows - mean
    var = jnp.mean(centered * centered, axis=-1, keepdims=True)
    return centered * lax.rsqrt(var + 1e-06) * gain


def dot(a, b, dims):
    return lax.dot_general(a, b, (dims, ((), ())), preferred_element_type=F32)


def attention(f, lengths_row, seg_len, rate, head):
    total = 64 * BLK
    index = jnp.arange(total, dtype=jnp.int32)
    ends = jnp.cumsum(lengths_row, dtype=jnp.int32)
    after = index[:, None] >= ends[None, :]
    slide = jnp.sum(after.astype(jnp.int32), axis=1, dtype=jnp.int32)
    start = jnp.sum(jnp.where(after, lengths_row[None, :], 0), axis=1, dtype=jnp.int32)
    size = jnp.sum(
        jnp.where(slide[:, None] == jnp.arange(3)[None, :], lengths_row[None, :], 0), axis=1
    )
    pos = index - start
    segment = pos // seg_len
    each = (lengths_row + seg_len - 1) // seg_len
    before = jnp.sum(jnp.where(after, each[None, :], 0), axis=1, dtype=jnp.int32)
    ident = before + segment
    picked = pos % rate == head % rate
    spots = jnp.arange(SEGS, dtype=jnp.int32)
    kid = jnp.where(picked, ident, -1).reshape(64, 1, BLK)
    kmask = jnp.where(kid == spots[None, :, None], 0.0, NEG).astype(BF)
    begin = start + segment * seg_len
    end = start + jnp.minimum(size, (segment + 1) * seg_len)
    section = lax.axis_index("section")

    def of_queries(values):
        values = values.reshape(16, 4, BLK)
        return lax.dynamic_index_in_dim(values, section, 1, keepdims=False).reshape(2048 // QT, QT)

    qid = of_queries(ident)[:, None, :]
    hot = (qid == spots[None, :, None]).astype(BF)
    free = of_queries(1.0 - picked.astype(F32))
    lo = jnp.min(of_queries(begin), axis=1) // (KT * UNROLL)
    hi = (jnp.max(of_queries(end), axis=1) + KT * UNROLL - 1) // (KT * UNROLL)
    spec = pltpu.PrefetchScalarGridSpec(
        num_scalar_prefetch=2,
        grid=(2048 // QT,),
        in_specs=[
            pl.BlockSpec((64, 3, HD, BLK), lambda t, lo, hi: (0, 0, 0, 0)),
            pl.BlockSpec((64, SEGS, BLK), lambda t, lo, hi: (0, 0, 0)),
            pl.BlockSpec((1, SEGS, QT), lambda t, lo, hi: (t, 0, 0)),
            pl.BlockSpec((2048 // QT, QT), lambda t, lo, hi: (0, 0)),
        ],
        out_specs=pl.BlockSpec((QT // BLK, HD, BLK), lambda t, lo, hi: (t, 0, 0)),
        scratch_shapes=[
            pltpu.VMEM((64, BLK, BLK), BF),
            pltpu.VMEM((64 // KB, 64, KT), BF),
        ],
    )
    return pl.pallas_call(
        attention_kernel,
        grid_spec=spec,
        out_shape=jax.ShapeDtypeStruct((16, HD, BLK), BF),
        compiler_params=pltpu.CompilerParams(dimension_semantics=("arbitrary",)),
    )(lo, hi, f.reshape(64, 3, HD, BLK), kmask, hot, free)


def per_device(
    tile_feats,
    tile_gain,
    w_gate,
    w_up,
    w_down,
    w_proj,
    slide_gain,
    w_qkv,
    w_out,
    lengths,
    seg_len,
    rate,
):
    section = lax.axis_index("section")
    seq = lax.axis_index("seq")
    xh, z = seq // NZ, seq % NZ
    xl = section // 2

    wq = w_qkv.transpose(0, 2, 1).reshape(576, 768)
    mine = tile_feats[0].reshape(2, 2, BLK, 384)
    wi = jnp.concatenate([seg_len, rate]).reshape(8, 1)
    wi = jnp.broadcast_to(jnp.pad(wi, ((0, 8), (0, 0))), (16, BLK))
    ga, gb, xs, gp, gq, go, gi = comm(
        gather_kernel,
        0,
        [
            ((2, NZ, NY, ROWS, 1024), BF),
            ((2, NZ, NY, ROWS, 2048), BF),
            ((2, 2, BLK, 1536), BF),
            ((4, 384, 768), BF),
            ((4, 576, 768), BF),
            ((4, 192, 768), BF),
            ((4, 16, BLK), jnp.int32),
        ],
        120,
        24,
        [
            pltpu.VMEM((3, ROWS, 512), BF),
            pltpu.VMEM((2, BLK, 384), BF),
            pltpu.VMEM((384, 768), BF),
            pltpu.VMEM((576, 768), BF),
            pltpu.VMEM((192, 768), BF),
            pltpu.VMEM((16, BLK), jnp.int32),
        ],
        w_gate,
        w_up,
        w_down.T,
        mine,
        w_proj,
        wq,
        w_out,
        wi,
    )
    rows = xs.reshape(4 * BLK, 1536)
    normed = layer_norm(rows.astype(F32), tile_gain).astype(BF)
    ga = ga.reshape(1536, 1024)
    gb = gb.reshape(1536, 2048)
    gate = dot(normed, ga, ((1,), (0,)))
    part = None
    for core in range(2):
        up = dot(normed, gb[:, core * 1024 : core * 1024 + 512], ((1,), (0,)))
        hidden = (jax.nn.silu(gate[:, core * 512 : core * 512 + 512]) * up).astype(BF)
        term = dot(hidden, gb[:, core * 1024 + 512 : core * 1024 + 1024], ((1,), (1,)))
        part = term if part is None else part + term
    part = part.astype(BF).reshape(2, 2, BLK, 1536)
    (others,) = comm(
        scatter_kernel,
        1,
        [((3, BLK, 1536), BF)],
        8,
        0,
        [pltpu.VMEM((2, BLK // 2, 1536), BF)],
        part,
    )
    own = part[xh, xl].astype(F32) + jnp.sum(others.astype(F32), axis=0)
    tile_out = (xs[xh, xl].astype(F32) + own).astype(BF)
    emb = dot(tile_out, gp.reshape(1536, 768), ((1,), (0,)))
    slide_normed = layer_norm(emb, slide_gain).astype(BF)
    qkv = dot(gq.reshape(2304, 768), slide_normed, ((1,), (1,))).astype(BF)
    (f,) = comm(
        heads_kernel,
        2,
        [((2, NZ, 2, 2, 3, HD, BLK), BF)],
        50,
        1,
        [pltpu.VMEM((NZ, 3, HD, BLK), BF)],
        qkv.reshape(4, 3, 4, HD, BLK),
        place=VM,
    )
    head = z * 2 + xh
    segs = gi[:, :4, 0].reshape(16)
    rates = gi[:, 4:8, 0].reshape(16)
    o = attention(f, lengths[0], segs[head], rates[head], head)
    (att,) = comm(back_kernel, 3, [((16, HD, BLK), BF)], 16, 1, [], o, place=VM)
    out = emb.T + dot(go.reshape(768, 768), att.reshape(768, BLK), ((0,), (0,)))
    out = out.astype(BF).reshape(4, 192, BLK)
    (full,) = comm(out_kernel, 4, [((192, 4 * BLK), BF)], 4, 1, [], out, place=VM)
    return full.T[None]


def solution(mesh):
    placed = (
        P("dp", "seq", "section"),
        P(),
        P(("seq", "dp"), "section"),
        P(("seq", "dp"), "section"),
        P("section", ("seq", "dp")),
        P("section", None),
        P(),
        P(None, None, "section"),
        P("section", None),
        P("dp", None),
        P("section"),
        P("section"),
    )
    return jax.shard_map(
        per_device, mesh=mesh, in_specs=placed, out_specs=P("dp", "seq", "section"), check_vma=False
    )
```

```python
import functools
import math

import jax
import jax.numpy as jnp
from jax import lax
from jax.experimental import pallas as pl
from jax.experimental.pallas import tpu as pltpu
from jax.sharding import PartitionSpec as P

MESH = pl.DeviceIdType.MESH
BF = jnp.bfloat16
F32 = jnp.float32
NZ = 8
NY = 4
ROWS = 24
BLK = 128
HD = 48
NEG = -(2.0**100)
SEGS = 32
ANY = pl.BlockSpec(memory_space=pl.ANY)
VM = pl.BlockSpec(memory_space=pltpu.VMEM)


def rem(a, n):
    return lax.rem(a, jnp.int32(n))


def div(a, n):
    return lax.div(a, jnp.int32(n))


class Place:
    def __init__(self):
        self.s = lax.axis_index("section")
        self.q = lax.axis_index("seq")
        self.y = lax.axis_index("dp")
        self.xl = div(self.s, 2)
        self.c = rem(self.s, 2)
        self.xh = div(self.q, NZ)
        self.z = rem(self.q, NZ)
        self.x = self.xh * 2 + self.xl

    def at(self, xh=None, xl=None, c=None, z=None, y=None):
        xh = self.xh if xh is None else xh
        xl = self.xl if xl is None else xl
        c = self.c if c is None else c
        z = self.z if z is None else z
        y = self.y if y is None else y
        return {"section": xl * 2 + c, "seq": xh * NZ + z, "dp": y}

    def zat(self, d):
        return self.at(z=rem(self.z + d + NZ, NZ))

    def yat(self, d):
        return self.at(y=rem(self.y + d + NY, NY))

    def xpos(self, d):
        x = rem(self.x + d + 4, 4)
        return div(x, 2), rem(x, 2)

    def xat(self, d, c=None):
        xh, xl = self.xpos(d)
        return self.at(xh=xh, xl=xl, c=c)


def greet(devices):
    barrier = pltpu.get_barrier_semaphore()
    for device in devices:
        pl.semaphore_signal(barrier, inc=1, device_id=device, device_id_type=MESH)
    pl.semaphore_wait(barrier, len(devices))


class Link:
    def __init__(self, send_sem, recv_sem, local_sem=None):
        self.send_sem, self.recv_sem, self.local_sem = send_sem, recv_sem, local_sem
        self.sent = []
        self.local = 0

    def remote(self, src, dst, device):
        n = len(self.sent)
        copy = pltpu.make_async_remote_copy(
            src_ref=src,
            dst_ref=dst,
            send_sem=self.send_sem.at[n],
            recv_sem=self.recv_sem.at[n],
            device_id=device,
            device_id_type=MESH,
        )
        copy.start()
        self.sent.append(copy)
        return copy

    def here(self, src, dst):
        copy = pltpu.make_async_copy(src, dst, self.local_sem.at[self.local])
        self.local += 1
        copy.start()
        return copy

    def finish(self):
        for copy in self.sent:
            copy.wait_send()


def gather_kernel(
    wg, wu, wd, mine, wp, wq, wo, wi, ga, gb, xs, gp, gq, go, gi,
    vw, vx, vp, vq, vo, vi, send_sem, recv_sem, local_sem
):
    me = Place()
    xh, xl, c, y, z, s = me.xh, me.xl, me.c, me.y, me.z, me.s
    other = 1 - c
    partner = me.at(c=other)
    across = me.at(xh=1 - xh)
    yp, ym, zp, zm = me.yat(1), me.yat(-1), me.zat(1), me.zat(-1)
    greet(
        [yp, ym, zp, zm, partner, across]
        + [me.xat(1), me.xat(1, other), me.xat(-1), me.xat(-1, other)]
    )
    link = Link(send_sem, recv_sem, local_sem)
    la = pl.ds(pl.multiple_of(c * 512, 512), 512)
    lb = pl.ds(pl.multiple_of(c * 1024, 1024), 1024)

    def yi(d):
        return rem(y + d + NY, NY)

    def zi(d):
        return rem(z + d + NZ, NZ)

    ex, lo = [], []

    def cols(half):
        return pl.ds(pl.multiple_of(half * 512, 512), 512)

    for n, (w, g, first) in enumerate(
        ((wg, ga, c * 512), (wu, gb, c * 1024), (wd, gb, c * 1024 + 512))
    ):
        spot = g.at[xh, z, y, :, pl.ds(pl.multiple_of(first, 512), 512)]
        ex.append(link.remote(w.at[:, cols(1 - xh)], spot, across))
        lo.append((link.here(w.at[:, cols(xh)], vw.at[n]), vw.at[n], spot))
    def feat(sec):
        return pl.ds(pl.multiple_of(sec * 384, 128), 384)

    x_direct = {}
    for d in (1, -1):
        for k in (0, 1):
            core = c if k == 0 else other
            x_direct[d, k] = link.remote(
                mine.at[:, core], xs.at[xh, :, :, feat(s)], me.xat(d, core)
            )
    x_pair = link.remote(mine.at[:, other], xs.at[xh, :, :, feat(s)], partner)
    x_in = link.here(mine.at[:, c], vx)
    small = ((wi, gi, vi), (wp, gp, vp), (wq, gq, vq), (wo, go, vo))
    small_in = [link.here(w, v) for w, g, v in small]
    lo_out = []
    for copy, via, spot in lo:
        copy.wait()
        lo_out.append(link.here(via, spot))
    for copy in ex:
        copy.wait_recv()
    for copy in lo_out:
        copy.wait()
    x_in.wait()
    x_own = link.here(vx, xs.at[xh, :, :, feat(s)])

    def gate_y(dst, yy, part=None):
        ref = ga.at[:, z, yy, :, la] if part is None else ga.at[part, z, yy, :, la]
        return link.remote(ref, ref, dst)

    def gate_z(dst, zz, part=None):
        ref = ga.at[:, zz, :, :, la] if part is None else ga.at[part, zz, :, :, la]
        return link.remote(ref, ref, dst)

    def rest(dst, zz, yy, part=None):
        ref = gb.at[:, zz, yy, :, lb] if part is None else gb.at[part, zz, yy, :, lb]
        return link.remote(ref, ref, dst)

    def pair_a(zz):
        ref = ga.at[:, zz, :, :, la]
        return link.remote(ref, ref, partner)

    def pair_b(zz):
        ref = gb.at[:, zz, :, :, lb]
        return link.remote(ref, ref, partner)

    pairs = []
    ay = {1: gate_y(yp, y), -1: gate_y(ym, y)}
    bz = {1: rest(zp, z, y), -1: rest(zm, z, y)}
    by, byo = {}, {}

    def spread(d):
        by[d] = (rest(yp, zi(d), y), rest(ym, zi(d), y))

    def pass_on(d):
        zz = zi(d)
        by[d][0].wait_recv()
        by[d][1].wait_recv()
        byo[d] = (rest(yp, zz, yi(-1), 0), rest(ym, zz, yi(1), 1))

    spread(0)
    ay[1].wait_recv()
    ay[-1].wait_recv()
    ayo = (gate_y(yp, yi(-1), 0), gate_y(ym, yi(1), 1))

    def hop_b(step):
        bz[1].wait_recv()
        bz[-1].wait_recv()
        part = (None, None) if step < 3 else (0, 1)
        if step < 4:
            bz[1] = rest(zp, zi(-step), y, part[0])
            bz[-1] = rest(zm, zi(step), y, part[1])
        spread(-step)
        if step < 4:
            spread(step)

    hop_b(1)
    ayo[0].wait_recv()
    ayo[1].wait_recv()
    az = {(d, p): gate_z(zp if d == 1 else zm, z, p) for p in (0, 1) for d in (1, -1)}
    pairs.append(pair_a(z))

    def hop_a(step):
        for p in (0, 1):
            for d in (1, -1):
                if step < 4 or (d, p) in ((1, 0), (-1, 1)):
                    az[d, p].wait_recv()
                if step < 3 or (step == 3 and (d, p) in ((1, 0), (-1, 1))):
                    az[d, p] = gate_z(zp if d == 1 else zm, zi(-step * d), p)
        pairs.append(pair_a(zi(-step)))
        if step < 4:
            pairs.append(pair_a(zi(step)))

    pass_on(0)
    hop_b(2)
    x_far = []
    for d in (1, -1):
        xxh, xxl = me.xpos(-d)
        row = 0 if d == 1 else 1
        for k in (0, 1):
            x_direct[d, k].wait_recv()
            sec = xxl * 2 + (c if k == 0 else other)
            ref = xs.at[xxh, row, :, feat(sec)]
            x_far.append(link.remote(ref, ref, me.xat(d)))
    sent_small = []
    for (w, g, v), copy in zip(small, small_in):
        half = w.shape[0] // 2
        up = link.remote(w.at[pl.ds(0, half)], g.at[s, pl.ds(0, half)], me.xat(1))
        dn = link.remote(w.at[pl.ds(half, half)], g.at[s, pl.ds(half, half)], me.xat(-1))
        own = link.remote(w, g.at[s], partner)
        copy.wait()
        sent_small.append((g, up, dn, own, link.here(v, g.at[s])))

    pass_on(-1)
    pass_on(1)
    hop_a(1)
    hop_b(3)
    pass_on(-2)
    pass_on(2)
    hop_a(2)
    hop_b(4)

    def whole(d):
        byo[d][0].wait_recv()
        byo[d][1].wait_recv()
        pairs.append(pair_b(zi(d)))

    pass_on(-3)
    pass_on(3)
    whole(0)
    hop_a(3)
    pass_on(-4)
    for d in (-1, 1, -2, 2):
        whole(d)
    hop_a(4)
    far = (1 - xl) * 2 + c

    def whole_small(n):
        g, up, dn, own, local = sent_small[n]
        up.wait_recv()
        dn.wait_recv()
        pairs.append(link.remote(g.at[far], g.at[far], partner))

    whole_small(0)
    whole_small(1)
    for d in (-3, 3, -4):
        whole(d)
    whole_small(2)
    whole_small(3)
    for g, up, dn, own, local in sent_small:
        own.wait_recv()
        local.wait()
    x_pair.wait_recv()
    x_own.wait()
    for copy in x_far + pairs:
        copy.wait_recv()
    link.finish()


def scatter_kernel(t, r, stage, send_sem, recv_sem):
    me = Place()
    xp, xm = me.xat(1), me.xat(-1)
    greet([xp, xm])
    link = Link(send_sem, recv_sem)
    h = BLK // 2

    def part(d):
        return me.xpos(d)

    oh, ol = part(2)
    first = link.remote(t.at[oh, ol, pl.ds(0, h)], stage.at[0], xp)
    second = link.remote(t.at[oh, ol, pl.ds(h, h)], stage.at[1], xm)
    ph, pw = part(1)
    mh, mw = part(-1)
    a = link.remote(t.at[ph, pw], r.at[0], xp)
    b = link.remote(t.at[mh, mw], r.at[1], xm)
    first.wait_recv()
    far0 = link.remote(stage.at[0], r.at[2, pl.ds(0, h)], xp)
    second.wait_recv()
    far1 = link.remote(stage.at[1], r.at[2, pl.ds(h, h)], xm)
    for copy in (a, b, far0, far1):
        copy.wait_recv()
    link.finish()


NEAR = (1, 7, 2, 6, 3, 5, 4)


def heads_kernel(qkv, f, stage, send_sem, recv_sem, local_sem):
    me = Place()
    xh, xl, c, z = me.xh, me.xl, me.c, me.z
    flip = me.at(xl=1 - xl)
    cross = me.at(xh=1 - xh, xl=1 - xl)
    partner = me.at(c=1 - c)
    greet([me.zat(d) for d in range(1, NZ)] + [flip, cross, partner])
    link = Link(send_sem, recv_sem, local_sem)
    kv = pl.ds(1, 2)

    def head(zz, e):
        n = zz * 2 + e
        return qkv.at[div(n, 4), :, rem(n, 4)]

    def head_kv(zz, e):
        n = zz * 2 + e
        return qkv.at[div(n, 4), kv, rem(n, 4)]

    def zi(d):
        return rem(z + d + NZ, NZ)

    keep, move = {}, {}
    own = link.here(head(z, xh), f.at[xh, z, xl, c])
    for d in NEAR:
        zz = zi(d)
        keep[d] = link.remote(head(zz, xh), f.at[xh, z, xl, c], me.zat(d))
        move[d] = link.remote(head(zz, 1 - xh), stage.at[z], me.zat(d))
    to_cross = {0: link.remote(head(z, 1 - xh), f.at[xh, z, xl, c], cross)}
    to_flip = {0: link.remote(head_kv(z, xh), f.at[xh, z, xl, c, kv], flip)}
    relay = {}

    def pass_on(d):
        to_cross[d].wait_recv()
        ref = f.at[1 - xh, zi(-d), 1 - xl, c]
        relay[d] = link.remote(ref, ref, flip)

    last = None
    for d in NEAR:
        zz = zi(-d)
        move[d].wait_recv()
        to_cross[d] = link.remote(stage.at[zz], f.at[xh, zz, xl, c], cross)
        keep[d].wait_recv()
        ref = f.at[xh, zz, xl, c, kv]
        to_flip[d] = link.remote(ref, ref, flip)
        if last is not None:
            pass_on(last)
        last = d if last is not None else 0
        if d == NEAR[1]:
            pass_on(NEAR[0])
            last = d
    pass_on(last)
    own.wait()
    pairs = []

    def pair(xxh, xxl):
        ref = f.at[xxh, :, xxl, c, kv]
        pairs.append(link.remote(ref, ref, partner))

    pair(xh, xl)
    for d in range(NZ):
        to_flip[d].wait_recv()
    pair(xh, 1 - xl)
    pair(1 - xh, 1 - xl)
    for d in range(NZ):
        relay[d].wait_recv()
    pair(1 - xh, xl)
    for copy in pairs:
        copy.wait_recv()
    link.finish()


def back_kernel(o, a, send_sem, recv_sem, local_sem):
    me = Place()
    xh, z = me.xh, me.z
    places = [(e, d) for e in (0, 1) for d in range(NZ) if (e, d) != (0, 0)]

    def target(e, d):
        zz = rem(z + d, NZ)
        xx = xh if e == 0 else 1 - xh
        return xx, zz

    devices = []
    for e, d in places:
        xx, zz = target(e, d)
        devices.append(me.at(xh=xx, z=zz))
    greet(devices)
    link = Link(send_sem, recv_sem, local_sem)
    head = z * 2 + xh
    for (e, d), device in zip(places, devices):
        xx, zz = target(e, d)
        link.remote(o.at[xx * NZ + zz], a.at[head], device)
    own = link.here(o.at[xh * NZ + z], a.at[head])
    for copy in list(link.sent):
        copy.wait_recv()
    own.wait()
    link.finish()


def out_kernel(o, full, send_sem, recv_sem, local_sem):
    me = Place()
    xl, c, s = me.xl, me.c, me.s
    here = pl.ds(pl.multiple_of(s * BLK, BLK), BLK)
    spots = [(xl, 1 - c), (1 - xl, c), (1 - xl, 1 - c)]
    greet([me.at(xl=a, c=b) for a, b in spots])
    link = Link(send_sem, recv_sem, local_sem)
    for a, b in spots:
        link.remote(o.at[a * 2 + b], full.at[:, here], me.at(xl=a, c=b))
    own = link.here(o.at[s], full.at[:, here])
    for copy in list(link.sent):
        copy.wait_recv()
    own.wait()
    link.finish()


QT = 512
KT = 256
UNROLL = 4
FFC = 256
KB = KT // BLK


def attention_kernel(len_ref, rule_ref, f_ref, o_ref, k_s, v_s):
    t = pl.program_id(0)
    s = lax.axis_index("section")
    seq = lax.axis_index("seq")
    head = rem(seq, NZ) * 2 + div(seq, NZ)
    seg = rule_ref[div(head, 4), rem(head, 4)]
    rate = rule_ref[div(head, 4), 4 + rem(head, 4)]
    sizes = [len_ref[0, n] for n in range(3)]
    first, second = sizes[0], sizes[0] + sizes[1]
    count = [lax.div(size + seg - 1, seg) for size in sizes[:2]]
    blocks = f_ref.shape[0]
    factor = math.log2(math.e) / math.sqrt(HD)
    lanes = lax.broadcasted_iota(jnp.int32, (1, BLK), 1)
    spots = lax.broadcasted_iota(jnp.int32, (SEGS, BLK), 0).astype(F32)

    def pick(index, a, b, c):
        return jnp.where(index >= second, c, jnp.where(index >= first, b, a))

    def place(start):
        index = lanes + start
        pos = (index - pick(index, 0, first, second)).astype(F32)
        base = pick(index, 0, count[0], count[0] + count[1]).astype(F32)
        width, step = seg.astype(F32), rate.astype(F32)
        ident = base + jnp.floor((pos + 0.5) / width)
        left = pos - step * jnp.floor((pos + 0.5) / step)
        return ident, left == lax.rem(head, rate).astype(F32)

    def span(index):
        start = pick(index, 0, first, second)
        size = pick(index, *sizes)
        begin = lax.div(index - start, seg) * seg
        return start + begin, start + jnp.minimum(size, begin + seg)

    @pl.when(t == 0)
    def _():
        v_s[:, HD:, :] = jnp.ones_like(v_s[:, HD:, :])

        def prep(n, carry):
            for j in range(KB):
                b = n * KB + j
                key = f_ref[b, 1]
                ident, picked = place(b * BLK)
                ident = jnp.where(picked, ident, -1.0)
                mask = jnp.where(ident == spots, 0.0, NEG).astype(BF)
                k_s[b] = jnp.concatenate([key, key, mask], axis=0).T
                v_s[n, :HD, j * BLK : (j + 1) * BLK] = f_ref[b, 2]
            return carry

        lax.fori_loop(0, blocks // KB, prep, 0)

    each = QT // BLK
    starts = [((t * each + j) * 4 + s) * BLK for j in range(each)]
    hots, frees = [], []
    for start in starts:
        ident, picked = place(start)
        hots.append(jnp.where(ident == spots, 1.0, 0.0))
        frees.append(jnp.where(picked, 0.0, 1.0))
    hot = jnp.concatenate(hots, axis=1).astype(BF)
    free = jnp.concatenate(frees, axis=1)
    low_key = span(starts[0])[0]
    high_key = span(starts[-1] + BLK - 1)[1]

    def mine(part):
        return jnp.concatenate(
            [f_ref[(t * each + j) * 4 + s, part].astype(F32) for j in range(each)], axis=1
        )

    scaled = mine(0) * factor
    high = scaled.astype(BF)
    low = (scaled - high.astype(F32)).astype(BF)
    query = jnp.concatenate([high, low, hot], axis=0)
    top = jnp.sum(scaled * mine(1), axis=0, keepdims=True)
    acc = jnp.concatenate(
        [mine(2) * free, jnp.broadcast_to(free, (v_s.shape[1] - HD, QT))], axis=0
    )

    def body(m, carry):
        top, acc = carry
        scores = []
        for u in range(UNROLL):
            n = m * UNROLL + u
            keys = k_s[pl.ds(n * KB, KB)].reshape(KT, BLK)
            scores.append(jnp.dot(keys, query, preferred_element_type=F32))
        for u in range(UNROLL):
            n = m * UNROLL + u
            fresh = jnp.maximum(top, jnp.max(scores[u], axis=0, keepdims=True))
            weights = jnp.exp2(scores[u] - fresh)
            acc = acc * jnp.exp2(top - fresh) + jnp.dot(
                v_s[n], weights.astype(BF), preferred_element_type=F32
            )
            top = fresh
        return top, acc

    top, acc = lax.fori_loop(
        lax.div(low_key, KT * UNROLL),
        lax.div(high_key + KT * UNROLL - 1, KT * UNROLL),
        body,
        (top, acc),
    )
    result = (acc[:HD] / acc[HD : HD + 1]).astype(BF)
    for j in range(QT // BLK):
        o_ref[j] = result[:, j * BLK : (j + 1) * BLK]


def sems(n):
    return [pltpu.SemaphoreType.DMA((n,)), pltpu.SemaphoreType.DMA((n,))]


def comm(kernel, ident, outs, copies, local, scratch, *args, place=ANY):
    extra = list(scratch) + sems(copies)
    if local:
        extra.append(pltpu.SemaphoreType.DMA((local,)))
    return pl.pallas_call(
        kernel,
        out_shape=[jax.ShapeDtypeStruct(shape, kind) for shape, kind in outs],
        in_specs=[place] * len(args),
        out_specs=[ANY] * len(outs),
        scratch_shapes=extra,
        compiler_params=pltpu.CompilerParams(collective_id=ident, has_side_effects=True),
    )(*args)


def layer_norm(rows, gain):
    mean = jnp.mean(rows, axis=-1, keepdims=True)
    centered = rows - mean
    var = jnp.mean(centered * centered, axis=-1, keepdims=True)
    return centered * lax.rsqrt(var + 1e-06) * gain


def dot(a, b, dims):
    return lax.dot_general(a, b, (dims, ((), ())), preferred_element_type=F32)


def attention(f, lengths, rules):
    spec = pltpu.PrefetchScalarGridSpec(
        num_scalar_prefetch=2,
        grid=(2048 // QT,),
        in_specs=[pl.BlockSpec((64, 3, HD, BLK), lambda t, a, b: (0, 0, 0, 0))],
        out_specs=pl.BlockSpec((QT // BLK, HD, BLK), lambda t, a, b: (t, 0, 0)),
        scratch_shapes=[
            pltpu.VMEM((64, BLK, BLK), BF),
            pltpu.VMEM((64 // KB, 64, KT), BF),
        ],
    )
    return pl.pallas_call(
        attention_kernel,
        grid_spec=spec,
        out_shape=jax.ShapeDtypeStruct((16, HD, BLK), BF),
        compiler_params=pltpu.CompilerParams(dimension_semantics=("arbitrary",)),
    )(lengths, rules, f.reshape(64, 3, HD, BLK))


def ffn_kernel(x_ref, gain_ref, wg_ref, wu_ref, wd_ref, o_ref, n_s, acc_s):
    n = pl.program_id(0)

    @pl.when(n == 0)
    def _():
        for r in range(4):
            rows = pl.ds(r * BLK, BLK)
            n_s[rows] = layer_norm(x_ref[rows].astype(F32), gain_ref[...]).astype(BF)

    normed = n_s[...]
    gate = jnp.dot(normed, wg_ref[...], preferred_element_type=F32)
    up = jnp.dot(normed, wu_ref[...], preferred_element_type=F32)
    hidden = (jax.nn.silu(gate) * up).astype(BF)
    term = dot(hidden, wd_ref[...], ((1,), (1,)))

    @pl.when(n == 0)
    def _():
        acc_s[...] = term

    @pl.when((n > 0) & (n < pl.num_programs(0) - 1))
    def _():
        acc_s[...] += term

    @pl.when(n == pl.num_programs(0) - 1)
    def _():
        o_ref[...] = (acc_s[...] + term).astype(BF)


def ffn(rows, gain, ga, gb):
    tokens, width = rows.shape
    steps = 1024 // FFC
    half = 512 // FFC

    def cols(kind):
        def index(n):
            return 0, (n // half) * 2 * half + kind * half + n % half

        return index

    def weights(index):
        return pl.BlockSpec((width, FFC), index)

    return pl.pallas_call(
        ffn_kernel,
        grid=(steps,),
        in_specs=[
            pl.BlockSpec((tokens, width), lambda n: (0, 0)),
            pl.BlockSpec((1, width), lambda n: (0, 0)),
            weights(lambda n: (0, n)),
            weights(cols(0)),
            weights(cols(1)),
        ],
        out_specs=pl.BlockSpec((tokens, width), lambda n: (0, 0)),
        out_shape=jax.ShapeDtypeStruct((tokens, width), BF),
        scratch_shapes=[pltpu.VMEM((tokens, width), BF), pltpu.VMEM((tokens, width), F32)],
        compiler_params=pltpu.CompilerParams(dimension_semantics=("arbitrary",)),
    )(rows, gain[None], ga, gb, gb)


def per_device(
    tile_feats,
    tile_gain,
    w_gate,
    w_up,
    w_down,
    w_proj,
    slide_gain,
    w_qkv,
    w_out,
    lengths,
    seg_len,
    rate,
):
    section = lax.axis_index("section")
    xh = lax.axis_index("seq") // NZ
    xl = section // 2

    wq = w_qkv.transpose(0, 2, 1).reshape(576, 768)
    mine = tile_feats[0].reshape(2, 2, BLK, 384)
    wi = jnp.concatenate([seg_len, rate]).reshape(8, 1)
    wi = jnp.broadcast_to(jnp.pad(wi, ((0, 8), (0, 0))), (16, BLK))
    ga, gb, xs, gp, gq, go, gi = comm(
        gather_kernel,
        0,
        [
            ((2, NZ, NY, ROWS, 1024), BF),
            ((2, NZ, NY, ROWS, 2048), BF),
            ((2, 2, BLK, 1536), BF),
            ((4, 384, 768), BF),
            ((4, 576, 768), BF),
            ((4, 192, 768), BF),
            ((4, 16, BLK), jnp.int32),
        ],
        120,
        24,
        [
            pltpu.VMEM((3, ROWS, 512), BF),
            pltpu.VMEM((2, BLK, 384), BF),
            pltpu.VMEM((384, 768), BF),
            pltpu.VMEM((576, 768), BF),
            pltpu.VMEM((192, 768), BF),
            pltpu.VMEM((16, BLK), jnp.int32),
        ],
        w_gate,
        w_up,
        w_down.T,
        mine,
        w_proj,
        wq,
        w_out,
        wi,
    )
    rows = xs.reshape(4 * BLK, 1536)
    part = ffn(rows, tile_gain, ga.reshape(1536, 1024), gb.reshape(1536, 2048))
    part = part.reshape(2, 2, BLK, 1536)
    (others,) = comm(
        scatter_kernel,
        1,
        [((3, BLK, 1536), BF)],
        8,
        0,
        [pltpu.VMEM((2, BLK // 2, 1536), BF)],
        part,
    )
    own = part[xh, xl].astype(F32) + jnp.sum(others.astype(F32), axis=0)
    tile_out = (xs[xh, xl].astype(F32) + own).astype(BF)
    emb = dot(tile_out, gp.reshape(1536, 768), ((1,), (0,)))
    slide_normed = layer_norm(emb, slide_gain).astype(BF)
    qkv = dot(gq.reshape(2304, 768), slide_normed, ((1,), (1,))).astype(BF)
    (f,) = comm(
        heads_kernel,
        2,
        [((2, NZ, 2, 2, 3, HD, BLK), BF)],
        50,
        1,
        [pltpu.VMEM((NZ, 3, HD, BLK), BF)],
        qkv.reshape(4, 3, 4, HD, BLK),
        place=VM,
    )
    o = attention(f, lengths, gi[:, :8, 0])
    (att,) = comm(back_kernel, 3, [((16, HD, BLK), BF)], 16, 1, [], o, place=VM)
    out = emb.T + dot(go.reshape(768, 768), att.reshape(768, BLK), ((0,), (0,)))
    out = out.astype(BF).reshape(4, 192, BLK)
    (full,) = comm(out_kernel, 4, [((192, 4 * BLK), BF)], 4, 1, [], out, place=VM)
    return full.T[None]


def solution(mesh):
    placed = (
        P("dp", "seq", "section"),
        P(),
        P(("seq", "dp"), "section"),
        P(("seq", "dp"), "section"),
        P("section", ("seq", "dp")),
        P("section", None),
        P(),
        P(None, None, "section"),
        P("section", None),
        P("dp", None),
        P("section"),
        P("section"),
    )
    return jax.shard_map(
        per_device, mesh=mesh, in_specs=placed, out_specs=P("dp", "seq", "section"), check_vma=False
    )
```

```python
import functools
import math

import jax
import jax.numpy as jnp
from jax import lax
from jax.experimental import pallas as pl
from jax.experimental.pallas import tpu as pltpu
from jax.sharding import PartitionSpec as P

MESH = pl.DeviceIdType.MESH
BF = jnp.bfloat16
F32 = jnp.float32
NZ = 8
NY = 4
ROWS = 24
BLK = 128
HD = 48
NEG = -(2.0**100)
SEGS = 32
ANY = pl.BlockSpec(memory_space=pl.ANY)
VM = pl.BlockSpec(memory_space=pltpu.VMEM)


def rem(a, n):
    return lax.rem(a, jnp.int32(n))


def div(a, n):
    return lax.div(a, jnp.int32(n))


class Place:
    def __init__(self):
        self.s = lax.axis_index("section")
        self.q = lax.axis_index("seq")
        self.y = lax.axis_index("dp")
        self.xl = div(self.s, 2)
        self.c = rem(self.s, 2)
        self.xh = div(self.q, NZ)
        self.z = rem(self.q, NZ)
        self.x = self.xh * 2 + self.xl

    def at(self, xh=None, xl=None, c=None, z=None, y=None):
        xh = self.xh if xh is None else xh
        xl = self.xl if xl is None else xl
        c = self.c if c is None else c
        z = self.z if z is None else z
        y = self.y if y is None else y
        return {"section": xl * 2 + c, "seq": xh * NZ + z, "dp": y}

    def zat(self, d):
        return self.at(z=rem(self.z + d + NZ, NZ))

    def yat(self, d):
        return self.at(y=rem(self.y + d + NY, NY))

    def xpos(self, d):
        x = rem(self.x + d + 4, 4)
        return div(x, 2), rem(x, 2)

    def xat(self, d, c=None):
        xh, xl = self.xpos(d)
        return self.at(xh=xh, xl=xl, c=c)


def greet(devices):
    barrier = pltpu.get_barrier_semaphore()
    for device in devices:
        pl.semaphore_signal(barrier, inc=1, device_id=device, device_id_type=MESH)
    pl.semaphore_wait(barrier, len(devices))


class Link:
    def __init__(self, send_sem, recv_sem, local_sem=None):
        self.send_sem, self.recv_sem, self.local_sem = send_sem, recv_sem, local_sem
        self.sent = []
        self.local = 0

    def remote(self, src, dst, device):
        n = len(self.sent)
        copy = pltpu.make_async_remote_copy(
            src_ref=src,
            dst_ref=dst,
            send_sem=self.send_sem.at[n],
            recv_sem=self.recv_sem.at[n],
            device_id=device,
            device_id_type=MESH,
        )
        copy.start()
        self.sent.append(copy)
        return copy

    def here(self, src, dst):
        copy = pltpu.make_async_copy(src, dst, self.local_sem.at[self.local])
        self.local += 1
        copy.start()
        return copy

    def finish(self):
        for copy in self.sent:
            copy.wait_send()


def gather_kernel(
    wg, wu, wd, mine, wp, wq, wo, wi, ga, gb, xs, gp, gq, go, gi,
    vw, vx, vp, vq, vo, vi, send_sem, recv_sem, local_sem
):
    me = Place()
    xh, xl, c, y, z, s = me.xh, me.xl, me.c, me.y, me.z, me.s
    other = 1 - c
    partner = me.at(c=other)
    across = me.at(xh=1 - xh)
    yp, ym, zp, zm = me.yat(1), me.yat(-1), me.zat(1), me.zat(-1)
    greet(
        [yp, ym, zp, zm, partner, across]
        + [me.xat(1), me.xat(1, other), me.xat(-1), me.xat(-1, other)]
    )
    link = Link(send_sem, recv_sem, local_sem)
    la = pl.ds(pl.multiple_of(c * 512, 512), 512)
    lb = pl.ds(pl.multiple_of(c * 1024, 1024), 1024)

    def yi(d):
        return rem(y + d + NY, NY)

    def zi(d):
        return rem(z + d + NZ, NZ)

    ex, lo = [], []

    def cols(half):
        return pl.ds(pl.multiple_of(half * 512, 512), 512)

    for n, (w, g, first) in enumerate(
        ((wg, ga, c * 512), (wu, gb, c * 1024), (wd, gb, c * 1024 + 512))
    ):
        spot = g.at[xh, z, y, :, pl.ds(pl.multiple_of(first, 512), 512)]
        ex.append(link.remote(w.at[:, cols(1 - xh)], spot, across))
        lo.append((link.here(w.at[:, cols(xh)], vw.at[n]), vw.at[n], spot))
    def feat(sec):
        return pl.ds(pl.multiple_of(sec * 384, 128), 384)

    x_direct = {}
    for d in (1, -1):
        for k in (0, 1):
            core = c if k == 0 else other
            x_direct[d, k] = link.remote(
                mine.at[:, core], xs.at[xh, :, :, feat(s)], me.xat(d, core)
            )
    x_pair = link.remote(mine.at[:, other], xs.at[xh, :, :, feat(s)], partner)
    x_in = link.here(mine.at[:, c], vx)
    small = ((wi, gi, vi), (wp, gp, vp), (wq, gq, vq), (wo, go, vo))
    small_in = [link.here(w, v) for w, g, v in small]
    lo_out = []
    for copy, via, spot in lo:
        copy.wait()
        lo_out.append(link.here(via, spot))
    for copy in ex:
        copy.wait_recv()
    for copy in lo_out:
        copy.wait()
    x_in.wait()
    x_own = link.here(vx, xs.at[xh, :, :, feat(s)])

    def gate_y(dst, yy, part=None):
        ref = ga.at[:, z, yy, :, la] if part is None else ga.at[part, z, yy, :, la]
        return link.remote(ref, ref, dst)

    def gate_z(dst, zz, part=None):
        ref = ga.at[:, zz, :, :, la] if part is None else ga.at[part, zz, :, :, la]
        return link.remote(ref, ref, dst)

    def rest(dst, zz, yy, part=None):
        ref = gb.at[:, zz, yy, :, lb] if part is None else gb.at[part, zz, yy, :, lb]
        return link.remote(ref, ref, dst)

    def pair_a(zz):
        ref = ga.at[:, zz, :, :, la]
        return link.remote(ref, ref, partner)

    def pair_b(zz):
        ref = gb.at[:, zz, :, :, lb]
        return link.remote(ref, ref, partner)

    pairs = []
    ay = {1: gate_y(yp, y), -1: gate_y(ym, y)}
    bz = {1: rest(zp, z, y), -1: rest(zm, z, y)}
    by, byo = {}, {}

    def spread(d):
        by[d] = (rest(yp, zi(d), y), rest(ym, zi(d), y))

    def pass_on(d):
        zz = zi(d)
        by[d][0].wait_recv()
        by[d][1].wait_recv()
        byo[d] = (rest(yp, zz, yi(-1), 0), rest(ym, zz, yi(1), 1))

    spread(0)
    ay[1].wait_recv()
    ay[-1].wait_recv()
    ayo = (gate_y(yp, yi(-1), 0), gate_y(ym, yi(1), 1))

    def hop_b(step):
        bz[1].wait_recv()
        bz[-1].wait_recv()
        part = (None, None) if step < 3 else (0, 1)
        if step < 4:
            bz[1] = rest(zp, zi(-step), y, part[0])
            bz[-1] = rest(zm, zi(step), y, part[1])
        spread(-step)
        if step < 4:
            spread(step)

    hop_b(1)
    ayo[0].wait_recv()
    ayo[1].wait_recv()
    az = {(d, p): gate_z(zp if d == 1 else zm, z, p) for p in (0, 1) for d in (1, -1)}
    pairs.append(pair_a(z))

    def hop_a(step):
        for p in (0, 1):
            for d in (1, -1):
                if step < 4 or (d, p) in ((1, 0), (-1, 1)):
                    az[d, p].wait_recv()
                if step < 3 or (step == 3 and (d, p) in ((1, 0), (-1, 1))):
                    az[d, p] = gate_z(zp if d == 1 else zm, zi(-step * d), p)
        pairs.append(pair_a(zi(-step)))
        if step < 4:
            pairs.append(pair_a(zi(step)))

    pass_on(0)
    hop_b(2)
    x_far = []
    for d in (1, -1):
        xxh, xxl = me.xpos(-d)
        row = 0 if d == 1 else 1
        for k in (0, 1):
            x_direct[d, k].wait_recv()
            sec = xxl * 2 + (c if k == 0 else other)
            ref = xs.at[xxh, row, :, feat(sec)]
            x_far.append(link.remote(ref, ref, me.xat(d)))
    sent_small = []
    for (w, g, v), copy in zip(small, small_in):
        half = w.shape[0] // 2
        up = link.remote(w.at[pl.ds(0, half)], g.at[s, pl.ds(0, half)], me.xat(1))
        dn = link.remote(w.at[pl.ds(half, half)], g.at[s, pl.ds(half, half)], me.xat(-1))
        own = link.remote(w, g.at[s], partner)
        copy.wait()
        sent_small.append((g, up, dn, own, link.here(v, g.at[s])))

    pass_on(-1)
    pass_on(1)
    hop_a(1)
    hop_b(3)
    pass_on(-2)
    pass_on(2)
    hop_a(2)
    hop_b(4)

    def whole(d):
        byo[d][0].wait_recv()
        byo[d][1].wait_recv()
        pairs.append(pair_b(zi(d)))

    pass_on(-3)
    pass_on(3)
    whole(0)
    hop_a(3)
    pass_on(-4)
    for d in (-1, 1, -2, 2):
        whole(d)
    hop_a(4)
    far = (1 - xl) * 2 + c

    def whole_small(n):
        g, up, dn, own, local = sent_small[n]
        up.wait_recv()
        dn.wait_recv()
        pairs.append(link.remote(g.at[far], g.at[far], partner))

    whole_small(0)
    whole_small(1)
    for d in (-3, 3, -4):
        whole(d)
    whole_small(2)
    whole_small(3)
    for g, up, dn, own, local in sent_small:
        own.wait_recv()
        local.wait()
    x_pair.wait_recv()
    x_own.wait()
    for copy in x_far + pairs:
        copy.wait_recv()
    link.finish()


def scatter_kernel(t, r, stage, total, send_sem, recv_sem):
    me = Place()
    xp, xm = me.xat(1), me.xat(-1)
    greet([xp, xm])
    link = Link(send_sem, recv_sem)
    low, high = pl.ds(0, BLK // 2), pl.ds(BLK // 2, BLK // 2)
    (oh, ol), (ph, pw), (mh, mw) = me.xpos(2), me.xpos(1), me.xpos(-1)
    first = link.remote(t.at[oh, ol, low], stage.at[0], xp)
    second = link.remote(t.at[oh, ol, high], stage.at[1], xm)
    plain = [
        link.remote(t.at[ph, pw, high], r.at[0, high], xp),
        link.remote(t.at[mh, mw, low], r.at[1, low], xm),
    ]
    first.wait_recv()
    total[0] = (t[ph, pw, low].astype(F32) + stage[0].astype(F32)).astype(BF)
    second.wait_recv()
    total[1] = (t[mh, mw, high].astype(F32) + stage[1].astype(F32)).astype(BF)
    sums = [
        link.remote(total.at[0], r.at[0, low], xp),
        link.remote(total.at[1], r.at[1, high], xm),
    ]
    for copy in plain + sums:
        copy.wait_recv()
    link.finish()


NEAR = (1, 7, 2, 6, 3, 5, 4)
LATE = (4,)


def heads_kernel(qkv, f, stage, send_sem, recv_sem, local_sem):
    me = Place()
    xh, xl, c, z = me.xh, me.xl, me.c, me.z
    flip = me.at(xl=1 - xl)
    cross = me.at(xh=1 - xh, xl=1 - xl)
    across = me.at(xh=1 - xh)
    partner = me.at(c=1 - c)
    greet([me.zat(d) for d in range(1, NZ)] + [flip, cross, across, partner])
    link = Link(send_sem, recv_sem, local_sem)
    kv = pl.ds(1, 2)

    def head(zz, e):
        n = zz * 2 + e
        return qkv.at[div(n, 4), :, rem(n, 4)]

    def head_kv(zz, e):
        n = zz * 2 + e
        return qkv.at[div(n, 4), kv, rem(n, 4)]

    def zi(d):
        return rem(z + d + NZ, NZ)

    keep, move = {}, {}
    own = link.here(head(z, xh), f.at[xh, z, xl, c])
    for d in NEAR:
        zz = zi(d)
        keep[d] = link.remote(head(zz, xh), f.at[xh, z, xl, c], me.zat(d))
        move[d] = link.remote(head(zz, 1 - xh), stage.at[z], me.zat(d))
    to_cross = {0: link.remote(head(z, 1 - xh), f.at[xh, z, xl, c], cross)}
    to_flip = {0: link.remote(head_kv(z, xh), f.at[xh, z, xl, c, kv], flip)}
    relay = {}

    def pass_on(d):
        to_cross[d].wait_recv()
        if d not in LATE:
            ref = f.at[1 - xh, zi(-d), 1 - xl, c]
            relay[d] = link.remote(ref, ref, flip)

    last = None
    for d in NEAR:
        zz = zi(-d)
        move[d].wait_recv()
        to_cross[d] = link.remote(stage.at[zz], f.at[xh, zz, xl, c], cross)
        if d in LATE:
            relay[d] = link.remote(stage.at[zz], f.at[xh, zz, xl, c], across)
        keep[d].wait_recv()
        ref = f.at[xh, zz, xl, c, kv]
        to_flip[d] = link.remote(ref, ref, flip)
        if last is not None:
            pass_on(last)
        last = d if last is not None else 0
        if d == NEAR[1]:
            pass_on(NEAR[0])
            last = d
    pass_on(last)
    own.wait()
    pairs = []

    def pair(xxh, xxl):
        ref = f.at[xxh, :, xxl, c, kv]
        pairs.append(link.remote(ref, ref, partner))

    pair(xh, xl)
    for d in range(NZ):
        to_flip[d].wait_recv()
    pair(xh, 1 - xl)
    pair(1 - xh, 1 - xl)
    for d in range(NZ):
        relay[d].wait_recv()
    pair(1 - xh, xl)
    for copy in pairs:
        copy.wait_recv()
    link.finish()


def back_kernel(o, a, send_sem, recv_sem, local_sem):
    me = Place()
    xh, z = me.xh, me.z
    places = [(e, d) for e in (0, 1) for d in range(NZ) if (e, d) != (0, 0)]

    def target(e, d):
        zz = rem(z + d, NZ)
        xx = xh if e == 0 else 1 - xh
        return xx, zz

    devices = []
    for e, d in places:
        xx, zz = target(e, d)
        devices.append(me.at(xh=xx, z=zz))
    greet(devices)
    link = Link(send_sem, recv_sem, local_sem)
    head = z * 2 + xh
    for (e, d), device in zip(places, devices):
        xx, zz = target(e, d)
        link.remote(o.at[xx * NZ + zz], a.at[head], device)
    own = link.here(o.at[xh * NZ + z], a.at[head])
    for copy in list(link.sent):
        copy.wait_recv()
    own.wait()
    link.finish()


def out_kernel(o, full, send_sem, recv_sem, local_sem):
    me = Place()
    xl, c, s = me.xl, me.c, me.s
    here = pl.ds(pl.multiple_of(s * BLK, BLK), BLK)
    spots = [(xl, 1 - c), (1 - xl, c), (1 - xl, 1 - c)]
    greet([me.at(xl=a, c=b) for a, b in spots])
    link = Link(send_sem, recv_sem, local_sem)
    for a, b in spots:
        link.remote(o.at[a * 2 + b], full.at[:, here], me.at(xl=a, c=b))
    own = link.here(o.at[s], full.at[:, here])
    for copy in list(link.sent):
        copy.wait_recv()
    own.wait()
    link.finish()


QT = 512
KT = 256
UNROLL = 4
FFC = 256
KB = KT // BLK


def attention_kernel(len_ref, rule_ref, f_ref, o_ref, k_s, v_s):
    t = pl.program_id(0)
    s = lax.axis_index("section")
    seq = lax.axis_index("seq")
    head = rem(seq, NZ) * 2 + div(seq, NZ)
    seg = rule_ref[div(head, 4), rem(head, 4)]
    rate = rule_ref[div(head, 4), 4 + rem(head, 4)]
    sizes = [len_ref[0, n] for n in range(3)]
    first, second = sizes[0], sizes[0] + sizes[1]
    count = [lax.div(size + seg - 1, seg) for size in sizes[:2]]
    blocks = f_ref.shape[0]
    factor = math.log2(math.e) / math.sqrt(HD)
    lanes = lax.broadcasted_iota(jnp.int32, (1, BLK), 1)
    spots = lax.broadcasted_iota(jnp.int32, (SEGS, BLK), 0).astype(F32)

    def pick(index, a, b, c):
        return jnp.where(index >= second, c, jnp.where(index >= first, b, a))

    def place(start):
        index = lanes + start
        pos = (index - pick(index, 0, first, second)).astype(F32)
        base = pick(index, 0, count[0], count[0] + count[1]).astype(F32)
        width, step = seg.astype(F32), rate.astype(F32)
        ident = base + jnp.floor((pos + 0.5) / width)
        left = pos - step * jnp.floor((pos + 0.5) / step)
        return ident, left == lax.rem(head, rate).astype(F32)

    def span(index):
        start = pick(index, 0, first, second)
        size = pick(index, *sizes)
        begin = lax.div(index - start, seg) * seg
        return start + begin, start + jnp.minimum(size, begin + seg)

    @pl.when(t == 0)
    def _():
        v_s[:, HD:, :] = jnp.ones_like(v_s[:, HD:, :])

        def prep(n, carry):
            for j in range(KB):
                b = n * KB + j
                key = f_ref[b, 1]
                ident, picked = place(b * BLK)
                ident = jnp.where(picked, ident, -1.0)
                mask = jnp.where(ident == spots, 0.0, NEG).astype(BF)
                k_s[b] = jnp.concatenate([key, key, mask], axis=0).T
                v_s[n, :HD, j * BLK : (j + 1) * BLK] = f_ref[b, 2]
            return carry

        lax.fori_loop(0, blocks // KB, prep, 0, unroll=8)

    each = QT // BLK
    starts = [((t * each + j) * 4 + s) * BLK for j in range(each)]
    hots, frees = [], []
    for start in starts:
        ident, picked = place(start)
        hots.append(jnp.where(ident == spots, 1.0, 0.0))
        frees.append(jnp.where(picked, 0.0, 1.0))
    hot = jnp.concatenate(hots, axis=1).astype(BF)
    free = jnp.concatenate(frees, axis=1)
    low_key = span(starts[0])[0]
    high_key = span(starts[-1] + BLK - 1)[1]

    def mine(part):
        return jnp.concatenate(
            [f_ref[(t * each + j) * 4 + s, part].astype(F32) for j in range(each)], axis=1
        )

    scaled = mine(0) * factor
    high = scaled.astype(BF)
    low = (scaled - high.astype(F32)).astype(BF)
    query = jnp.concatenate([high, low, hot], axis=0)
    top = jnp.sum(scaled * mine(1), axis=0, keepdims=True)
    acc = jnp.concatenate(
        [mine(2) * free, jnp.broadcast_to(free, (v_s.shape[1] - HD, QT))], axis=0
    )

    def body(m, carry):
        top, acc = carry
        scores = []
        for u in range(UNROLL):
            n = m * UNROLL + u
            keys = k_s[pl.ds(n * KB, KB)].reshape(KT, BLK)
            scores.append(jnp.dot(keys, query, preferred_element_type=F32))
        for u in range(UNROLL):
            n = m * UNROLL + u
            fresh = jnp.maximum(top, jnp.max(scores[u], axis=0, keepdims=True))
            weights = jnp.exp2(scores[u] - fresh)
            acc = acc * jnp.exp2(top - fresh) + jnp.dot(
                v_s[n], weights.astype(BF), preferred_element_type=F32
            )
            top = fresh
        return top, acc

    top, acc = lax.fori_loop(
        lax.div(low_key, KT * UNROLL),
        lax.div(high_key + KT * UNROLL - 1, KT * UNROLL),
        body,
        (top, acc),
    )
    result = (acc[:HD] / acc[HD : HD + 1]).astype(BF)
    for j in range(QT // BLK):
        o_ref[j] = result[:, j * BLK : (j + 1) * BLK]


def sems(n):
    return [pltpu.SemaphoreType.DMA((n,)), pltpu.SemaphoreType.DMA((n,))]


def comm(kernel, ident, outs, copies, local, scratch, *args, place=ANY, out=ANY):
    extra = list(scratch) + sems(copies)
    if local:
        extra.append(pltpu.SemaphoreType.DMA((local,)))
    return pl.pallas_call(
        kernel,
        out_shape=[jax.ShapeDtypeStruct(shape, kind) for shape, kind in outs],
        in_specs=[place] * len(args),
        out_specs=[out] * len(outs),
        scratch_shapes=extra,
        compiler_params=pltpu.CompilerParams(collective_id=ident, has_side_effects=True),
    )(*args)


def layer_norm(rows, gain):
    mean = jnp.mean(rows, axis=-1, keepdims=True)
    centered = rows - mean
    var = jnp.mean(centered * centered, axis=-1, keepdims=True)
    return centered * lax.rsqrt(var + 1e-06) * gain


def dot(a, b, dims):
    return lax.dot_general(a, b, (dims, ((), ())), preferred_element_type=F32)


def attention(f, lengths, rules):
    spec = pltpu.PrefetchScalarGridSpec(
        num_scalar_prefetch=2,
        grid=(2048 // QT,),
        in_specs=[pl.BlockSpec((64, 3, HD, BLK), lambda t, a, b: (0, 0, 0, 0))],
        out_specs=pl.BlockSpec((QT // BLK, HD, BLK), lambda t, a, b: (t, 0, 0)),
        scratch_shapes=[
            pltpu.VMEM((64, BLK, BLK), BF),
            pltpu.VMEM((64 // KB, 64, KT), BF),
        ],
    )
    return pl.pallas_call(
        attention_kernel,
        grid_spec=spec,
        out_shape=jax.ShapeDtypeStruct((16, HD, BLK), BF),
        compiler_params=pltpu.CompilerParams(dimension_semantics=("arbitrary",)),
    )(lengths, rules, f.reshape(64, 3, HD, BLK))


def ffn_kernel(x_ref, gain_ref, wg_ref, wu_ref, wd_ref, o_ref, n_s, acc_s):
    n = pl.program_id(0)

    @pl.when(n == 0)
    def _():
        for r in range(4):
            rows = pl.ds(r * BLK, BLK)
            n_s[rows] = layer_norm(x_ref[rows].astype(F32), gain_ref[...][None]).astype(BF)

    normed = n_s[...]
    gate = jnp.dot(normed, wg_ref[...], preferred_element_type=F32)
    up = jnp.dot(normed, wu_ref[...], preferred_element_type=F32)
    hidden = (jax.nn.silu(gate) * up).astype(BF)
    term = dot(hidden, wd_ref[...], ((1,), (1,)))

    @pl.when(n == 0)
    def _():
        acc_s[...] = term

    @pl.when((n > 0) & (n < pl.num_programs(0) - 1))
    def _():
        acc_s[...] += term

    @pl.when(n == pl.num_programs(0) - 1)
    def _():
        o_ref[...] = (acc_s[...] + term).astype(BF)


def ffn(rows, gain, ga, gb):
    tokens, width = rows.shape
    steps = 1024 // FFC
    half = 512 // FFC

    def cols(kind):
        def index(n):
            return 0, (n // half) * 2 * half + kind * half + n % half

        return index

    def weights(index):
        return pl.BlockSpec((width, FFC), index)

    return pl.pallas_call(
        ffn_kernel,
        grid=(steps,),
        in_specs=[
            pl.BlockSpec((tokens, width), lambda n: (0, 0)),
            pl.BlockSpec((width,), lambda n: (0,)),
            weights(lambda n: (0, n)),
            weights(cols(0)),
            weights(cols(1)),
        ],
        out_specs=pl.BlockSpec((tokens, width), lambda n: (0, 0)),
        out_shape=jax.ShapeDtypeStruct((tokens, width), BF),
        scratch_shapes=[pltpu.VMEM((tokens, width), BF), pltpu.VMEM((tokens, width), F32)],
        compiler_params=pltpu.CompilerParams(dimension_semantics=("arbitrary",)),
    )(rows, gain, ga, gb, gb)


def scatter(part):
    (others,) = comm(
        scatter_kernel,
        1,
        [((2, BLK, 1536), BF)],
        8,
        0,
        [pltpu.VMEM((2, BLK // 2, 1536), BF)] * 2,
        part,
        place=VM,
    )
    return others


def heads(qkv):
    (f,) = comm(
        heads_kernel,
        2,
        [((2, NZ, 2, 2, 3, HD, BLK), BF)],
        50,
        1,
        [pltpu.VMEM((NZ, 3, HD, BLK), BF)],
        qkv,
        place=VM,
        out=VM,
    )
    return f


def per_device(
    tile_feats,
    tile_gain,
    w_gate,
    w_up,
    w_down,
    w_proj,
    slide_gain,
    w_qkv,
    w_out,
    lengths,
    seg_len,
    rate,
):
    section = lax.axis_index("section")
    xh = lax.axis_index("seq") // NZ
    xl = section // 2

    wq = w_qkv.transpose(0, 2, 1).reshape(576, 768)
    mine = tile_feats[0].reshape(2, 2, BLK, 384)
    wi = jnp.pad(jnp.concatenate([seg_len, rate]), (0, BLK - 8))
    wi = jnp.broadcast_to(wi[None], (16, BLK))
    ga, gb, xs, gp, gq, go, gi = comm(
        gather_kernel,
        0,
        [
            ((2, NZ, NY, ROWS, 1024), BF),
            ((2, NZ, NY, ROWS, 2048), BF),
            ((2, 2, BLK, 1536), BF),
            ((4, 384, 768), BF),
            ((4, 576, 768), BF),
            ((4, 192, 768), BF),
            ((4, 16, BLK), jnp.int32),
        ],
        120,
        24,
        [
            pltpu.VMEM((3, ROWS, 512), BF),
            pltpu.VMEM((2, BLK, 384), BF),
            pltpu.VMEM((384, 768), BF),
            pltpu.VMEM((576, 768), BF),
            pltpu.VMEM((192, 768), BF),
            pltpu.VMEM((16, BLK), jnp.int32),
        ],
        w_gate,
        w_up,
        w_down.T,
        mine,
        w_proj,
        wq,
        w_out,
        wi,
    )
    rows = xs.reshape(4 * BLK, 1536)
    part = ffn(rows, tile_gain, ga.reshape(1536, 1024), gb.reshape(1536, 2048))
    part = part.reshape(2, 2, BLK, 1536)
    others = scatter(part)
    own = part[xh, xl].astype(F32) + jnp.sum(others.astype(F32), axis=0)
    tile_out = (xs[xh, xl].astype(F32) + own).astype(BF)
    emb = dot(tile_out, gp.reshape(1536, 768), ((1,), (0,)))
    slide_normed = layer_norm(emb, slide_gain).astype(BF)
    qkv = dot(gq.reshape(2304, 768), slide_normed, ((1,), (1,))).astype(BF)
    f = heads(qkv.reshape(4, 3, 4, HD, BLK))
    o = attention(f, lengths, gi[:, 0, :8])
    (att,) = comm(back_kernel, 3, [((16, HD, BLK), BF)], 16, 1, [], o, place=VM)
    out = emb.T + dot(go.reshape(768, 768), att.reshape(768, BLK), ((0,), (0,)))
    out = out.astype(BF).reshape(4, 192, BLK)
    (full,) = comm(out_kernel, 4, [((192, 4 * BLK), BF)], 4, 1, [], out, place=VM)
    return full.T[None]


def solution(mesh):
    placed = (
        P("dp", "seq", "section"),
        P(),
        P(("seq", "dp"), "section"),
        P(("seq", "dp"), "section"),
        P("section", ("seq", "dp")),
        P("section", None),
        P(),
        P(None, None, "section"),
        P("section", None),
        P("dp", None),
        P("section"),
        P("section"),
    )
    return jax.shard_map(
        per_device, mesh=mesh, in_specs=placed, out_specs=P("dp", "seq", "section"), check_vma=False
    )
```

```python
import functools
import math

import jax
import jax.numpy as jnp
from jax import lax
from jax.experimental import pallas as pl
from jax.experimental.pallas import tpu as pltpu
from jax.sharding import PartitionSpec as P

MESH = pl.DeviceIdType.MESH
BF = jnp.bfloat16
F32 = jnp.float32
NZ = 8
NY = 4
ROWS = 24
BLK = 128
HD = 48
NEG = -(2.0**100)
SEGS = 32
ANY = pl.BlockSpec(memory_space=pl.ANY)
VM = pl.BlockSpec(memory_space=pltpu.VMEM)


def rem(a, n):
    return lax.rem(a, jnp.int32(n))


def div(a, n):
    return lax.div(a, jnp.int32(n))


class Place:
    def __init__(self):
        self.s = lax.axis_index("section")
        self.q = lax.axis_index("seq")
        self.y = lax.axis_index("dp")
        self.xl = div(self.s, 2)
        self.c = rem(self.s, 2)
        self.xh = div(self.q, NZ)
        self.z = rem(self.q, NZ)
        self.x = self.xh * 2 + self.xl

    def at(self, xh=None, xl=None, c=None, z=None, y=None):
        xh = self.xh if xh is None else xh
        xl = self.xl if xl is None else xl
        c = self.c if c is None else c
        z = self.z if z is None else z
        y = self.y if y is None else y
        return {"section": xl * 2 + c, "seq": xh * NZ + z, "dp": y}

    def zat(self, d):
        return self.at(z=rem(self.z + d + NZ, NZ))

    def yat(self, d):
        return self.at(y=rem(self.y + d + NY, NY))

    def xpos(self, d):
        x = rem(self.x + d + 4, 4)
        return div(x, 2), rem(x, 2)

    def xat(self, d, c=None):
        xh, xl = self.xpos(d)
        return self.at(xh=xh, xl=xl, c=c)


def greet(devices):
    barrier = pltpu.get_barrier_semaphore()
    for device in devices:
        pl.semaphore_signal(barrier, inc=1, device_id=device, device_id_type=MESH)
    pl.semaphore_wait(barrier, len(devices))


class Link:
    def __init__(self, send_sem, recv_sem, local_sem=None):
        self.send_sem, self.recv_sem, self.local_sem = send_sem, recv_sem, local_sem
        self.sent = []
        self.local = 0

    def remote(self, src, dst, device):
        n = len(self.sent)
        copy = pltpu.make_async_remote_copy(
            src_ref=src,
            dst_ref=dst,
            send_sem=self.send_sem.at[n],
            recv_sem=self.recv_sem.at[n],
            device_id=device,
            device_id_type=MESH,
        )
        copy.start()
        self.sent.append(copy)
        return copy

    def here(self, src, dst):
        copy = pltpu.make_async_copy(src, dst, self.local_sem.at[self.local])
        self.local += 1
        copy.start()
        return copy

    def finish(self):
        for copy in self.sent:
            copy.wait_send()


def gather_kernel(
    wg, wu, wd, mine, wp, wq, wi, ga, gb, xs, gp, gq, gi,
    vw, vx, vp, vq, vi, send_sem, recv_sem, local_sem
):
    me = Place()
    xh, xl, c, y, z, s = me.xh, me.xl, me.c, me.y, me.z, me.s
    other = 1 - c
    partner = me.at(c=other)
    across = me.at(xh=1 - xh)
    yp, ym, zp, zm = me.yat(1), me.yat(-1), me.zat(1), me.zat(-1)
    greet(
        [yp, ym, zp, zm, partner, across]
        + [me.xat(1), me.xat(1, other), me.xat(-1), me.xat(-1, other)]
    )
    link = Link(send_sem, recv_sem, local_sem)
    la = pl.ds(pl.multiple_of(c * 512, 512), 512)
    lb = pl.ds(pl.multiple_of(c * 1024, 1024), 1024)

    def yi(d):
        return rem(y + d + NY, NY)

    def zi(d):
        return rem(z + d + NZ, NZ)

    ex, lo = [], []

    def cols(half):
        return pl.ds(pl.multiple_of(half * 512, 512), 512)

    for n, (w, g, first) in enumerate(
        ((wg, ga, c * 512), (wu, gb, c * 1024), (wd, gb, c * 1024 + 512))
    ):
        spot = g.at[xh, z, y, :, pl.ds(pl.multiple_of(first, 512), 512)]
        ex.append(link.remote(w.at[:, cols(1 - xh)], spot, across))
        lo.append((link.here(w.at[:, cols(xh)], vw.at[n]), vw.at[n], spot))
    def feat(sec):
        return pl.ds(pl.multiple_of(sec * 384, 128), 384)

    x_direct = {}
    for d in (1, -1):
        for k in (0, 1):
            core = c if k == 0 else other
            x_direct[d, k] = link.remote(
                mine.at[:, core], xs.at[xh, :, :, feat(s)], me.xat(d, core)
            )
    x_pair = link.remote(mine.at[:, other], xs.at[xh, :, :, feat(s)], partner)
    x_in = link.here(mine.at[:, c], vx)
    small = ((wi, gi, vi), (wq, gq, vq), (wp, gp, vp))
    small_in = [link.here(w, v) for w, g, v in small]
    lo_out = []
    for copy, via, spot in lo:
        copy.wait()
        lo_out.append(link.here(via, spot))
    for copy in ex:
        copy.wait_recv()
    for copy in lo_out:
        copy.wait()
    x_in.wait()
    x_own = link.here(vx, xs.at[xh, :, :, feat(s)])

    def gate_y(dst, yy, part=None):
        ref = ga.at[:, z, yy, :, la] if part is None else ga.at[part, z, yy, :, la]
        return link.remote(ref, ref, dst)

    def gate_z(dst, zz, part=None):
        ref = ga.at[:, zz, :, :, la] if part is None else ga.at[part, zz, :, :, la]
        return link.remote(ref, ref, dst)

    def rest(dst, zz, yy, part=None):
        ref = gb.at[:, zz, yy, :, lb] if part is None else gb.at[part, zz, yy, :, lb]
        return link.remote(ref, ref, dst)

    def pair_a(zz):
        ref = ga.at[:, zz, :, :, la]
        return link.remote(ref, ref, partner)

    def pair_b(zz):
        ref = gb.at[:, zz, :, :, lb]
        return link.remote(ref, ref, partner)

    pairs = []
    ay = {1: gate_y(yp, y), -1: gate_y(ym, y)}
    bz = {1: rest(zp, z, y), -1: rest(zm, z, y)}
    by, byo = {}, {}

    def spread(d):
        by[d] = (rest(yp, zi(d), y), rest(ym, zi(d), y))

    def pass_on(d):
        zz = zi(d)
        by[d][0].wait_recv()
        by[d][1].wait_recv()
        byo[d] = (rest(yp, zz, yi(-1), 0), rest(ym, zz, yi(1), 1))

    spread(0)
    ay[1].wait_recv()
    ay[-1].wait_recv()
    ayo = (gate_y(yp, yi(-1), 0), gate_y(ym, yi(1), 1))

    def hop_b(step):
        bz[1].wait_recv()
        bz[-1].wait_recv()
        part = (None, None) if step < 3 else (0, 1)
        if step < 4:
            bz[1] = rest(zp, zi(-step), y, part[0])
            bz[-1] = rest(zm, zi(step), y, part[1])
        spread(-step)
        if step < 4:
            spread(step)

    hop_b(1)
    ayo[0].wait_recv()
    ayo[1].wait_recv()
    az = {(d, p): gate_z(zp if d == 1 else zm, z, p) for p in (0, 1) for d in (1, -1)}
    pairs.append(pair_a(z))

    def hop_a(step):
        for p in (0, 1):
            for d in (1, -1):
                if step < 4 or (d, p) in ((1, 0), (-1, 1)):
                    az[d, p].wait_recv()
                if step < 3 or (step == 3 and (d, p) in ((1, 0), (-1, 1))):
                    az[d, p] = gate_z(zp if d == 1 else zm, zi(-step * d), p)
        pairs.append(pair_a(zi(-step)))
        if step < 4:
            pairs.append(pair_a(zi(step)))

    pass_on(0)
    hop_b(2)
    x_far = []
    for d in (1, -1):
        xxh, xxl = me.xpos(-d)
        row = 0 if d == 1 else 1
        for k in (0, 1):
            x_direct[d, k].wait_recv()
            sec = xxl * 2 + (c if k == 0 else other)
            ref = xs.at[xxh, row, :, feat(sec)]
            x_far.append(link.remote(ref, ref, me.xat(d)))
    sent_small = []
    for (w, g, v), copy in zip(small, small_in):
        half = w.shape[0] // 2
        up = link.remote(w.at[pl.ds(0, half)], g.at[s, pl.ds(0, half)], me.xat(1))
        dn = link.remote(w.at[pl.ds(half, half)], g.at[s, pl.ds(half, half)], me.xat(-1))
        own = link.remote(w, g.at[s], partner)
        copy.wait()
        sent_small.append((g, up, dn, own, link.here(v, g.at[s])))

    pass_on(-1)
    pass_on(1)
    hop_a(1)
    hop_b(3)
    pass_on(-2)
    pass_on(2)
    hop_a(2)
    hop_b(4)

    def whole(d):
        byo[d][0].wait_recv()
        byo[d][1].wait_recv()
        pairs.append(pair_b(zi(d)))

    pass_on(-3)
    pass_on(3)
    whole(0)
    hop_a(3)
    pass_on(-4)
    for d in (-1, 1, -2, 2):
        whole(d)
    hop_a(4)
    far = (1 - xl) * 2 + c

    def whole_small(n):
        g, up, dn, own, local = sent_small[n]
        up.wait_recv()
        dn.wait_recv()
        pairs.append(link.remote(g.at[far], g.at[far], partner))

    whole_small(0)
    whole_small(1)
    for d in (-3, 3, -4):
        whole(d)
    whole_small(2)
    for g, up, dn, own, local in sent_small:
        own.wait_recv()
        local.wait()
    x_pair.wait_recv()
    x_own.wait()
    for copy in x_far + pairs:
        copy.wait_recv()
    link.finish()


def scatter_kernel(t, r, stage, total, send_sem, recv_sem):
    me = Place()
    xp, xm = me.xat(1), me.xat(-1)
    greet([xp, xm])
    link = Link(send_sem, recv_sem)
    low, high = pl.ds(0, BLK // 2), pl.ds(BLK // 2, BLK // 2)
    (oh, ol), (ph, pw), (mh, mw) = me.xpos(2), me.xpos(1), me.xpos(-1)
    first = link.remote(t.at[oh, ol, low], stage.at[0], xp)
    second = link.remote(t.at[oh, ol, high], stage.at[1], xm)
    plain = [
        link.remote(t.at[ph, pw, high], r.at[0, high], xp),
        link.remote(t.at[mh, mw, low], r.at[1, low], xm),
    ]
    first.wait_recv()
    total[0] = (t[ph, pw, low].astype(F32) + stage[0].astype(F32)).astype(BF)
    second.wait_recv()
    total[1] = (t[mh, mw, high].astype(F32) + stage[1].astype(F32)).astype(BF)
    sums = [
        link.remote(total.at[0], r.at[0, low], xp),
        link.remote(total.at[1], r.at[1, high], xm),
    ]
    for copy in plain + sums:
        copy.wait_recv()
    link.finish()


NEAR = (1, 7, 2, 6, 3, 5, 4)
LATE = (4,)


def heads_kernel(qkv, wo, f, go, stage, send_sem, recv_sem, local_sem):
    me = Place()
    xh, xl, c, z = me.xh, me.xl, me.c, me.z
    flip = me.at(xl=1 - xl)
    cross = me.at(xh=1 - xh, xl=1 - xl)
    across = me.at(xh=1 - xh)
    partner = me.at(c=1 - c)
    greet([me.zat(d) for d in range(1, NZ)] + [flip, cross, across, partner])
    link = Link(send_sem, recv_sem, local_sem)
    kv = pl.ds(1, 2)

    def head(zz, e):
        n = zz * 2 + e
        return qkv.at[div(n, 4), :, rem(n, 4)]

    def head_kv(zz, e):
        n = zz * 2 + e
        return qkv.at[div(n, 4), kv, rem(n, 4)]

    def zi(d):
        return rem(z + d + NZ, NZ)

    half = pl.ds(0, wo.shape[0] // 2), pl.ds(wo.shape[0] // 2, wo.shape[0] // 2)
    s, far = me.s, (1 - xl) * 2 + c
    out_up = link.remote(wo.at[half[0]], go.at[s, half[0]], me.xat(1))
    out_dn = link.remote(wo.at[half[1]], go.at[s, half[1]], me.xat(-1))
    out_own = link.remote(wo, go.at[s], partner)
    out_here = link.here(wo, go.at[s])
    keep, move = {}, {}
    own = link.here(head(z, xh), f.at[xh, z, xl, c])
    for d in NEAR:
        zz = zi(d)
        keep[d] = link.remote(head(zz, xh), f.at[xh, z, xl, c], me.zat(d))
        move[d] = link.remote(head(zz, 1 - xh), stage.at[z], me.zat(d))
    to_cross = {0: link.remote(head(z, 1 - xh), f.at[xh, z, xl, c], cross)}
    to_flip = {0: link.remote(head_kv(z, xh), f.at[xh, z, xl, c, kv], flip)}
    relay = {}

    def pass_on(d):
        to_cross[d].wait_recv()
        if d not in LATE:
            ref = f.at[1 - xh, zi(-d), 1 - xl, c]
            relay[d] = link.remote(ref, ref, flip)

    last = None
    for d in NEAR:
        zz = zi(-d)
        move[d].wait_recv()
        to_cross[d] = link.remote(stage.at[zz], f.at[xh, zz, xl, c], cross)
        if d in LATE:
            relay[d] = link.remote(stage.at[zz], f.at[xh, zz, xl, c], across)
        keep[d].wait_recv()
        ref = f.at[xh, zz, xl, c, kv]
        to_flip[d] = link.remote(ref, ref, flip)
        if last is not None:
            pass_on(last)
        last = d if last is not None else 0
        if d == NEAR[1]:
            pass_on(NEAR[0])
            last = d
    pass_on(last)
    own.wait()
    pairs = []

    def pair(xxh, xxl):
        ref = f.at[xxh, :, xxl, c, kv]
        pairs.append(link.remote(ref, ref, partner))

    pair(xh, xl)
    out_up.wait_recv()
    out_dn.wait_recv()
    pairs.append(link.remote(go.at[far], go.at[far], partner))
    out_own.wait_recv()
    out_here.wait()
    for d in range(NZ):
        to_flip[d].wait_recv()
    pair(xh, 1 - xl)
    pair(1 - xh, 1 - xl)
    for d in range(NZ):
        relay[d].wait_recv()
    pair(1 - xh, xl)
    for copy in pairs:
        copy.wait_recv()
    link.finish()


def back_kernel(o, a, send_sem, recv_sem, local_sem):
    me = Place()
    xh, z = me.xh, me.z
    places = [(e, d) for e in (0, 1) for d in range(NZ) if (e, d) != (0, 0)]

    def target(e, d):
        zz = rem(z + d, NZ)
        xx = xh if e == 0 else 1 - xh
        return xx, zz

    devices = []
    for e, d in places:
        xx, zz = target(e, d)
        devices.append(me.at(xh=xx, z=zz))
    greet(devices)
    link = Link(send_sem, recv_sem, local_sem)
    head = z * 2 + xh
    for (e, d), device in zip(places, devices):
        xx, zz = target(e, d)
        link.remote(o.at[xx * NZ + zz], a.at[head], device)
    own = link.here(o.at[xh * NZ + z], a.at[head])
    for copy in list(link.sent):
        copy.wait_recv()
    own.wait()
    link.finish()


def out_kernel(o, full, send_sem, recv_sem, local_sem):
    me = Place()
    xl, c, s = me.xl, me.c, me.s
    here = pl.ds(pl.multiple_of(s * BLK, BLK), BLK)
    spots = [(xl, 1 - c), (1 - xl, c), (1 - xl, 1 - c)]
    greet([me.at(xl=a, c=b) for a, b in spots])
    link = Link(send_sem, recv_sem, local_sem)
    for a, b in spots:
        link.remote(o.at[a * 2 + b], full.at[:, here], me.at(xl=a, c=b))
    own = link.here(o.at[s], full.at[:, here])
    for copy in list(link.sent):
        copy.wait_recv()
    own.wait()
    link.finish()


QT = 512
KT = 256
UNROLL = 4
FFC = 256
FFR = 256
KB = KT // BLK


def attention_kernel(len_ref, rule_ref, f_ref, o_ref, k_s, v_s):
    t = pl.program_id(0)
    s = lax.axis_index("section")
    seq = lax.axis_index("seq")
    head = rem(seq, NZ) * 2 + div(seq, NZ)
    seg = rule_ref[div(head, 4), 0, rem(head, 4)]
    rate = rule_ref[div(head, 4), 0, 4 + rem(head, 4)]
    sizes = [len_ref[0, n] for n in range(3)]
    first, second = sizes[0], sizes[0] + sizes[1]
    amount = [lax.div(size + seg - 1, seg) for size in sizes[:2]]
    blocks = f_ref.shape[0]
    factor = math.log2(math.e) / math.sqrt(HD)
    lanes = lax.broadcasted_iota(jnp.int32, (1, BLK), 1)
    spots = lax.broadcasted_iota(jnp.int32, (SEGS, BLK), 0).astype(F32)

    def pick(index, a, b, c):
        return jnp.where(index >= second, c, jnp.where(index >= first, b, a))

    def place(start):
        index = lanes + start
        pos = (index - pick(index, 0, first, second)).astype(F32)
        base = pick(index, 0, amount[0], amount[0] + amount[1]).astype(F32)
        width, step = seg.astype(F32), rate.astype(F32)
        ident = base + jnp.floor((pos + 0.5) / width)
        left = pos - step * jnp.floor((pos + 0.5) / step)
        return ident, left == lax.rem(head, rate).astype(F32)

    def span(index):
        start = pick(index, 0, first, second)
        size = pick(index, *sizes)
        begin = lax.div(index - start, seg) * seg
        return start + begin, start + jnp.minimum(size, begin + seg)

    @pl.when(t == 0)
    def _():
        v_s[:, HD:, :] = jnp.ones_like(v_s[:, HD:, :])

        def prep(n, carry):
            for j in range(KB):
                b = n * KB + j
                key = f_ref[b, 1]
                ident, picked = place(b * BLK)
                ident = jnp.where(picked, ident, -1.0)
                mask = jnp.where(ident == spots, 0.0, NEG).astype(BF)
                k_s[b] = jnp.concatenate([key, key, mask], axis=0).T
                v_s[n, :HD, j * BLK : (j + 1) * BLK] = f_ref[b, 2]
            return carry

        lax.fori_loop(0, blocks // KB, prep, 0, unroll=8)

    each = QT // BLK
    starts = [((t * each + j) * 4 + s) * BLK for j in range(each)]
    hots, frees = [], []
    for start in starts:
        ident, picked = place(start)
        hots.append(jnp.where(ident == spots, 1.0, 0.0))
        frees.append(jnp.where(picked, 0.0, 1.0))
    hot = jnp.concatenate(hots, axis=1).astype(BF)
    free = jnp.concatenate(frees, axis=1)
    low_key = span(starts[0])[0]
    high_key = span(starts[-1] + BLK - 1)[1]

    def mine(part):
        return jnp.concatenate(
            [f_ref[(t * each + j) * 4 + s, part].astype(F32) for j in range(each)], axis=1
        )

    scaled = mine(0) * factor
    high = scaled.astype(BF)
    low = (scaled - high.astype(F32)).astype(BF)
    query = jnp.concatenate([high, low, hot], axis=0)
    top = jnp.sum(scaled * mine(1), axis=0, keepdims=True)
    acc = jnp.concatenate(
        [mine(2) * free, jnp.broadcast_to(free, (v_s.shape[1] - HD, QT))], axis=0
    )

    def some(start, unroll, carry):
        top, acc = carry
        scores = []
        for u in range(unroll):
            keys = k_s[pl.ds((start + u) * KB, KB)].reshape(KT, BLK)
            scores.append(jnp.dot(keys, query, preferred_element_type=F32))
        for u in range(unroll):
            fresh = jnp.maximum(top, jnp.max(scores[u], axis=0, keepdims=True))
            weights = jnp.exp2(scores[u] - fresh)
            acc = acc * jnp.exp2(top - fresh) + jnp.dot(
                v_s[start + u], weights.astype(BF), preferred_element_type=F32
            )
            top = fresh
        return top, acc

    begin = lax.div(low_key, KT)
    count = lax.div(high_key + KT - 1, KT) - begin
    whole = lax.div(count, UNROLL)
    carry = lax.fori_loop(
        0, whole, lambda m, carry: some(begin + m * UNROLL, UNROLL, carry), (top, acc)
    )
    rest = begin + whole * UNROLL
    top, acc = lax.fori_loop(
        0, count - whole * UNROLL, lambda m, carry: some(rest + m, 1, carry), carry
    )
    result = (acc[:HD] / acc[HD : HD + 1]).astype(BF)
    for j in range(QT // BLK):
        o_ref[j] = result[:, j * BLK : (j + 1) * BLK]


def sems(n):
    return [pltpu.SemaphoreType.DMA((n,)), pltpu.SemaphoreType.DMA((n,))]


def comm(kernel, ident, outs, copies, local, scratch, *args, place=ANY, out=ANY):
    extra = list(scratch) + sems(copies)
    if local:
        extra.append(pltpu.SemaphoreType.DMA((local,)))
    return pl.pallas_call(
        kernel,
        out_shape=[jax.ShapeDtypeStruct(shape, kind) for shape, kind in outs],
        in_specs=[place] * len(args),
        out_specs=out if isinstance(out, list) else [out] * len(outs),
        scratch_shapes=extra,
        compiler_params=pltpu.CompilerParams(collective_id=ident, has_side_effects=True),
    )(*args)


def layer_norm(rows, gain):
    mean = jnp.mean(rows, axis=-1, keepdims=True)
    centered = rows - mean
    var = jnp.mean(centered * centered, axis=-1, keepdims=True)
    return centered * lax.rsqrt(var + 1e-06) * gain


def dot(a, b, dims):
    return lax.dot_general(a, b, (dims, ((), ())), preferred_element_type=F32)


def attention(f, lengths, rules):
    spec = pltpu.PrefetchScalarGridSpec(
        num_scalar_prefetch=2,
        grid=(2048 // QT,),
        in_specs=[pl.BlockSpec((64, 3, HD, BLK), lambda t, a, b: (0, 0, 0, 0))],
        out_specs=pl.BlockSpec((QT // BLK, HD, BLK), lambda t, a, b: (t, 0, 0)),
        scratch_shapes=[
            pltpu.VMEM((64, BLK, BLK), BF),
            pltpu.VMEM((64 // KB, 64, KT), BF),
        ],
    )
    return pl.pallas_call(
        attention_kernel,
        grid_spec=spec,
        out_shape=jax.ShapeDtypeStruct((16, HD, BLK), BF),
        compiler_params=pltpu.CompilerParams(dimension_semantics=("arbitrary",)),
    )(lengths, rules, f.reshape(64, 3, HD, BLK))


def ffn_kernel(x_ref, gain_ref, wg_ref, wu_ref, wd_ref, o_ref, n_s, acc_s):
    n = pl.program_id(0)

    def term(normed):
        gate = jnp.dot(normed, wg_ref[...], preferred_element_type=F32)
        up = jnp.dot(normed, wu_ref[...], preferred_element_type=F32)
        hidden = (jax.nn.silu(gate) * up).astype(BF)
        return dot(hidden, wd_ref[...], ((1,), (1,)))

    @pl.when(n == 0)
    def _():
        for r in range(0, x_ref.shape[0], FFR):
            rows = pl.ds(r, FFR)
            normed = layer_norm(x_ref[rows].astype(F32), gain_ref[...][None]).astype(BF)
            n_s[rows] = normed
            acc_s[rows] = term(normed)

    @pl.when((n > 0) & (n < pl.num_programs(0) - 1))
    def _():
        acc_s[...] += term(n_s[...])

    @pl.when(n == pl.num_programs(0) - 1)
    def _():
        o_ref[...] = (acc_s[...] + term(n_s[...])).astype(BF)


def ffn(rows, gain, ga, gb):
    tokens, width = rows.shape
    steps = 1024 // FFC
    half = 512 // FFC

    def cols(kind):
        def index(n):
            return 0, (n // half) * 2 * half + kind * half + n % half

        return index

    def weights(index):
        return pl.BlockSpec((width, FFC), index)

    return pl.pallas_call(
        ffn_kernel,
        grid=(steps,),
        in_specs=[
            pl.BlockSpec((tokens, width), lambda n: (0, 0)),
            pl.BlockSpec((width,), lambda n: (0,)),
            weights(lambda n: (0, n)),
            weights(cols(0)),
            weights(cols(1)),
        ],
        out_specs=pl.BlockSpec((tokens, width), lambda n: (0, 0)),
        out_shape=jax.ShapeDtypeStruct((tokens, width), BF),
        scratch_shapes=[pltpu.VMEM((tokens, width), BF), pltpu.VMEM((tokens, width), F32)],
        compiler_params=pltpu.CompilerParams(dimension_semantics=("arbitrary",)),
    )(rows, gain, ga, gb, gb)


def scatter(part):
    (others,) = comm(
        scatter_kernel,
        1,
        [((2, BLK, 1536), BF)],
        8,
        0,
        [pltpu.VMEM((2, BLK // 2, 1536), BF)] * 2,
        part,
        place=VM,
    )
    return others


def heads(qkv, w_out):
    return comm(
        heads_kernel,
        2,
        [((2, NZ, 2, 2, 3, HD, BLK), BF), ((4, 192, 768), BF)],
        50,
        2,
        [pltpu.VMEM((NZ, 3, HD, BLK), BF)],
        qkv,
        w_out,
        place=VM,
        out=[VM, ANY],
    )


def per_device(
    tile_feats,
    tile_gain,
    w_gate,
    w_up,
    w_down,
    w_proj,
    slide_gain,
    w_qkv,
    w_out,
    lengths,
    seg_len,
    rate,
):
    section = lax.axis_index("section")
    xh = lax.axis_index("seq") // NZ
    xl = section // 2

    wq = w_qkv.transpose(0, 2, 1).reshape(576, 768)
    mine = tile_feats[0].reshape(2, 2, BLK, 384)
    wi = jnp.pad(jnp.concatenate([seg_len, rate]), (0, BLK - 8))
    wi = jnp.broadcast_to(wi[None], (16, BLK))
    ga, gb, xs, gp, gq, gi = comm(
        gather_kernel,
        0,
        [
            ((2, NZ, NY, ROWS, 1024), BF),
            ((2, NZ, NY, ROWS, 2048), BF),
            ((2, 2, BLK, 1536), BF),
            ((4, 384, 768), BF),
            ((4, 576, 768), BF),
            ((4, 16, BLK), jnp.int32),
        ],
        120,
        24,
        [
            pltpu.VMEM((3, ROWS, 512), BF),
            pltpu.VMEM((2, BLK, 384), BF),
            pltpu.VMEM((384, 768), BF),
            pltpu.VMEM((576, 768), BF),
            pltpu.VMEM((16, BLK), jnp.int32),
        ],
        w_gate,
        w_up,
        w_down.T,
        mine,
        w_proj,
        wq,
        wi,
    )
    rows = xs.reshape(4 * BLK, 1536)
    part = ffn(rows, tile_gain, ga.reshape(1536, 1024), gb.reshape(1536, 2048))
    part = part.reshape(2, 2, BLK, 1536)
    others = scatter(part)
    own = part[xh, xl].astype(F32) + jnp.sum(others.astype(F32), axis=0)
    tile_out = (xs[xh, xl].astype(F32) + own).astype(BF)
    emb = dot(tile_out, gp.reshape(1536, 768), ((1,), (0,)))
    slide_normed = layer_norm(emb, slide_gain).astype(BF)
    qkv = dot(gq.reshape(2304, 768), slide_normed, ((1,), (1,))).astype(BF)
    f, go = heads(qkv.reshape(4, 3, 4, HD, BLK), w_out)
    o = attention(f, lengths, gi)
    (att,) = comm(back_kernel, 3, [((16, HD, BLK), BF)], 16, 1, [], o, place=VM)
    out = emb.T + dot(go.reshape(768, 768), att.reshape(768, BLK), ((0,), (0,)))
    out = out.astype(BF).reshape(4, 192, BLK)
    (full,) = comm(out_kernel, 4, [((192, 4 * BLK), BF)], 4, 1, [], out, place=VM)
    return full.T[None]


def solution(mesh):
    placed = (
        P("dp", "seq", "section"),
        P(),
        P(("seq", "dp"), "section"),
        P(("seq", "dp"), "section"),
        P("section", ("seq", "dp")),
        P("section", None),
        P(),
        P(None, None, "section"),
        P("section", None),
        P("dp", None),
        P("section"),
        P("section"),
    )
    return jax.shard_map(
        per_device, mesh=mesh, in_specs=placed, out_specs=P("dp", "seq", "section"), check_vma=False
    )
```
